128 devices in a mesh: req: 8 (over y, core), mlp: 16 (over x, z).
Axes of the slice: x: 4, y: 4, z: 4, core: 2. Of those that a mesh axis runs over, the one named last changes fastest.
Arguments:
- hidden_in: bfloat16 [1024, 2048], P('req', 'mlp'), may hold values from -6 to 6
- draft_len: int32 [64], P('req'), may hold values from 1 to 16, as said below
- accepted: int32 [64], P('req'), may hold values from 0 to 16, as said below
- pos_offset: int32 [64], P('req'), may hold values from 0 to 2047
- owner: int32 [64], replicated, may hold values from 0 to 63, as said below
- init_state: bfloat16 [2, 64, 256, 4096], P(None, 'req', None, 'mlp'), may hold values from -4 to 4
- norm_gain: float32 [2, 2, 2048], replicated, may hold values from 0.5 to 1.5
- w_query: bfloat16 [2, 2048, 2048], P(None, None, 'mlp'), may hold values from -0.125 to 0.125
- w_key: bfloat16 [2, 2048, 2048], P(None, None, 'mlp'), may hold values from -0.125 to 0.125
- w_value: bfloat16 [2, 2048, 4096], P(None, None, 'mlp')
- w_gate: bfloat16 [2, 2048, 4096], P(None, None, 'mlp'), may hold values from -0.125 to 0.125
- w_out: bfloat16 [2, 4096, 2048], P(None, 'mlp'), may hold values from -0.125 to 0.125
- w_up: bfloat16 [2, 2048, 4096], P(None, None, 'mlp'), may hold values from -0.125 to 0.125
- w_down: bfloat16 [2, 4096, 2048], P(None, 'mlp'), may hold values from -0.125 to 0.125
Outputs:
- hidden_out: bfloat16 [1024, 2048], P('req', 'mlp')
- new_state: bfloat16 [2, 64, 256, 4096], P(None, 'req', 'mlp')
The draws below stay inside these ranges and needn't reach their ends.
Inputs may be any that keep to these rules, and one draw needn't show every extreme that they name: `draft_len`: 16 and 1 both occur. `accepted`: at most the request's draft length; 0 and 16 both occur. `owner`: a permutation of the 64 slots; slot s belongs to index s // 8 of req; the requests of one index of req go to exactly half of the indices of req, exactly 2 to each.
All inputs are finite; a program needn't handle non-finite values.
Results may differ from the reference program's by a relative error of at most 0.035.
Values may be sent and summed in bfloat16 or wider, within the bound.
No kernel may reach another device: no remote copies, remote signals or barrier semaphores. Data moves between devices by JAX's collectives and lax.ppermute only.
A program may use at most 64 MiB of HBM per device.

```python
import math
import jax
import jax.numpy as jnp
from jax import lax

D = 2048
H = 8
K = 256
V = 512
FF = 4096
LAYERS = 2
MAXLEN = 16
R_DEV = 8
R = 64
CAP = 2
TOKENS = 1024
N_MLP = 16


def lengths_pair(key):
    folded = jax.random.fold_in(key, 11)
    key_one, key_two, key_three = jax.random.split(folded, 3)
    drafts = jax.random.randint(key_one, (R,), 1, MAXLEN + 1)
    ranking = jax.random.permutation(key_two, R)
    drafts = drafts.at[ranking[0]].set(MAXLEN).at[ranking[1]].set(1)
    accepts = jax.random.randint(key_three, (R,), 0, drafts + 1)
    accepts = accepts.at[ranking[0]].set(MAXLEN).at[ranking[2]].set(0)
    return (drafts.astype(jnp.int32), accepts.astype(jnp.int32))


def draw_draft_len(key, part):
    return lengths_pair(key)[0]


def draw_accepted(key, part):
    return lengths_pair(key)[1]


def draw_owner(key, part):
    groups = R // R_DEV
    key_one, key_two, key_three = jax.random.split(jax.random.fold_in(key, 29), 3)
    ranking = jax.vmap(lambda sub_key: jax.random.permutation(sub_key, R_DEV))(jax.random.split(key_one, groups))
    offsets = jax.random.permutation(key_two, groups)
    places = jax.vmap(lambda sub_key: jax.random.permutation(sub_key, R_DEV))(jax.random.split(key_three, groups))
    target = (ranking // CAP + offsets[:, None]) % groups
    slot_index = places[target, ranking]
    return (target * R_DEV + slot_index).reshape(R).astype(jnp.int32)


def draw_w_value(key, part):
    key_one, key_two = jax.random.split(jax.random.fold_in(key, 43), 2)
    columns = H * V
    channel = (jnp.arange(columns) % V).astype(jnp.float32)
    rough = jax.random.uniform(key_two, (LAYERS, 1, columns), jnp.float32, 0.5, 2.0)
    base = jnp.clip(jax.random.normal(key_one, (LAYERS, D, columns), jnp.float32), -6.0, 6.0)
    scales = jnp.exp((channel / V - 0.5) * math.log(10.0))[None, None, :] * rough
    return (base * scales * D ** (-0.5)).astype(jnp.bfloat16)


def set_ends(drawn, own_key, least, largest):
    shape = drawn.shape
    place = [jax.random.randint(jax.random.fold_in(own_key, axis), (), 0, shape[axis]) for axis in range(len(shape))]
    drawn = drawn.at[tuple(place)].set(least)
    longest = shape.index(max(shape))
    place[longest] = (place[longest] + 1) % shape[longest]
    return drawn.at[tuple(place)].set(largest)


def raised(result, stream_key, source, target, blocks, factor):
    owner, partner = [(jnp.arange(result.shape[axis_at]) // (result.shape[axis_at] // blocks)).reshape([-1 if axis == axis_at else 1 for axis in range(result.ndim)]) for axis_at in (source, target)]
    chosen = jax.random.permutation(stream_key, blocks)[partner]
    strong = (owner == chosen) | (owner == (partner + blocks // 2) % blocks)
    return jnp.where(strong, factor * result, result)


def block_scale(own_key, shape, cuts, least, high):
    gain, own = 1.0, jax.random.fold_in(own_key, 6)
    for axis_at, shards_of in cuts:
        steps = jnp.exp(jax.random.uniform(jax.random.fold_in(own, axis_at), (shards_of,), jnp.float32, least / len(cuts), high / len(cuts)))
        gain = gain * jnp.repeat(steps, shape[axis_at] // shards_of).reshape([-1 if axis == axis_at else 1 for axis in range(len(shape))])
    return gain


def bell_draw(rng, shape, scale, reach, pieces=(), kind=jnp.bfloat16):
    result = jax.random.normal(rng, shape, jnp.float32) * scale
    if len(pieces) > 0:
        result = block_scale(rng, shape, pieces, -0.22, 0.18) * result
    return jnp.clip(result, min=-reach, max=reach).astype(kind)


def heavy_noise(key, extent, deviation, most, shards, heavy, held_as=jnp.bfloat16):
    drawn = deviation * jax.random.normal(key, extent, jnp.float32)
    if shards:
        drawn = drawn * block_scale(key, extent, shards, -0.22, 0.18)
    return jnp.clip(raised(drawn, jax.random.fold_in(key, 3), *heavy), -most, most).astype(held_as)


def setup_inputs(seed: int = 0) -> dict:
    seeds = jax.random.split(jax.random.key(seed), 15)
    return {
        "hidden_in": bell_draw(seeds[0], (TOKENS, D), 1.0, 6.0, ((0, 8), (1, 16))),
        "draft_len": draw_draft_len(jax.random.fold_in(seeds[14], 71), 0),
        "accepted": draw_accepted(jax.random.fold_in(seeds[14], 71), 0),
        "pos_offset": set_ends(jax.random.randint(seeds[3], (R,), 0, 2048), jax.random.fold_in(seeds[3], 1), 0, 2047).astype(jnp.int32),
        "owner": draw_owner(jax.random.fold_in(seeds[14], 71), 0),
        "init_state": bell_draw(seeds[5], (LAYERS, R, K, H * V), 0.25, 4.0, ((1, 8), (3, 16))),
        "norm_gain": jnp.clip(1.0 + 0.1 * jax.random.normal(seeds[6], (LAYERS, 2, D), jnp.float32), 0.5, 1.5),
        "w_query": bell_draw(seeds[7], (LAYERS, D, H * K), D ** -0.5, 0.125, ((2, 16),)),
        "w_key": bell_draw(seeds[8], (LAYERS, D, H * K), D ** -0.5, 0.125, ((2, 16),)),
        "w_value": draw_w_value(jax.random.fold_in(seeds[14], 71), 0),
        "w_gate": bell_draw(seeds[10], (LAYERS, D, H * V), D ** -0.5, 0.125, ((2, 16),)),
        "w_out": heavy_noise(seeds[11], (LAYERS, H * V, D), (H * V) ** -0.5, 0.125, ((1, 16),), (1, 2, 16, 2.0)),
        "w_up": bell_draw(seeds[12], (LAYERS, D, FF), D ** -0.5, 0.125, ((2, 16),)),
        "w_down": heavy_noise(seeds[13], (LAYERS, FF, D), FF ** -0.5, 0.125, ((1, 16),), (1, 2, 16, 2.0)),
    }


EPSILON = 1e-05
HIGHEST = lax.Precision.HIGHEST

def layer_norm(values, scales):
    widened = values.astype(jnp.float32)
    center = lax.optimization_barrier(jnp.mean(widened, axis=-1, keepdims=True))
    shifted = widened - center
    spread = lax.optimization_barrier(jnp.mean(shifted * shifted, axis=-1, keepdims=True))
    return (shifted * lax.rsqrt(spread + EPSILON) * scales).astype(jnp.bfloat16)

def rotate(vectors, positions):
    halfway = vectors.shape[-1] // 2
    frequencies = jnp.exp(jnp.arange(halfway, dtype=jnp.float32) * (-math.log(10000.0) / halfway))
    angles = positions[..., None] * frequencies
    cosine = jnp.cos(angles)
    sine_part = jnp.sin(angles)
    first_half = vectors[..., :halfway]
    second = vectors[..., halfway:]
    return jnp.concatenate([first_half * cosine - second * sine_part, second * cosine + first_half * sine_part], axis=-1)

def reference(hidden_in, draft_len, accepted, pos_offset, owner, init_state, norm_gain, w_query, w_key, w_value, w_gate, w_out, w_up, w_down):
    decays = 1.0 - jnp.exp2(-5.0 - jnp.arange(H, dtype=jnp.float32))
    slot_steps = jnp.arange(MAXLEN, dtype=jnp.int32)
    positions = (pos_offset[:, None] + slot_steps[None, :]).reshape(TOKENS, 1).astype(jnp.float32)
    valid_rows = (slot_steps[None, :] < draft_len[:, None]).reshape(TOKENS)
    block_cols = H * V // N_MLP
    hidden_block = FF // N_MLP

    def run_request(packed):
        queries, keys_in, values_in, memory, taken_count = packed
        memory = memory.astype(jnp.float32).reshape(K, H, V)

        def advance(carried, inputs):
            current, chosen = carried
            query_now, key_now, value_now, step_index = inputs
            current = decays[None, :, None] * current + key_now.T[:, :, None] * value_now[None, :, :]
            output = jnp.einsum('hk,khv->hv', query_now, current, precision=HIGHEST)
            chosen = jnp.where(step_index + 1 == taken_count, current, chosen)
            return ((current, chosen), output)
        start_choice = jnp.where(taken_count == 0, memory, jnp.zeros_like(memory))
        (final_state, chosen), outputs = lax.scan(advance, (memory, start_choice), (queries, keys_in, values_in, slot_steps))
        return (outputs, chosen.reshape(K, H * V).astype(jnp.bfloat16))
    stream = hidden_in
    new_states = []
    for layer_index in range(LAYERS):
        normed = layer_norm(stream, norm_gain[layer_index, 0])
        queries = jnp.dot(normed, w_query[layer_index], preferred_element_type=jnp.float32).reshape(TOKENS, H, K)
        keys_all = jnp.dot(normed, w_key[layer_index], preferred_element_type=jnp.float32).reshape(TOKENS, H, K)
        queries = rotate(queries, positions)
        keys_all = rotate(keys_all, positions) * K ** (-0.5)
        values_all = jnp.dot(normed, w_value[layer_index], preferred_element_type=jnp.float32).reshape(TOKENS, H, V)
        gate_values = jnp.dot(normed, w_gate[layer_index], preferred_element_type=jnp.float32)
        outputs, chosen = lax.map(run_request, (queries.reshape(R, MAXLEN, H, K), keys_all.reshape(R, MAXLEN, H, K), values_all.reshape(R, MAXLEN, H, V), init_state[layer_index], accepted))
        retained = outputs.reshape(TOKENS, H, V)
        center = lax.optimization_barrier(jnp.mean(retained, axis=-1, keepdims=True))
        spread = lax.optimization_barrier(jnp.mean(retained * retained, axis=-1, keepdims=True)) - center * center
        normalized = ((retained - center) * lax.rsqrt(spread + EPSILON)).reshape(TOKENS, H * V)
        mixed_in = (normalized * jax.nn.silu(gate_values)).astype(jnp.bfloat16)
        attended = jnp.zeros((TOKENS, D), jnp.float32)
        for piece_index in range(N_MLP):
            first_col = piece_index * block_cols
            partial_value = jnp.dot(mixed_in[:, first_col:first_col + block_cols], w_out[layer_index, first_col:first_col + block_cols], preferred_element_type=jnp.float32)
            attended = attended + lax.optimization_barrier(partial_value.astype(jnp.bfloat16)).astype(jnp.float32)
        middle = (stream.astype(jnp.float32) + attended).astype(jnp.bfloat16)
        normed_mid = layer_norm(middle, norm_gain[layer_index, 1])
        hidden_units = jax.nn.gelu(jnp.dot(normed_mid, w_up[layer_index], preferred_element_type=jnp.float32), approximate=False).astype(jnp.bfloat16)
        feed_sum = jnp.zeros((TOKENS, D), jnp.float32)
        for piece_index in range(N_MLP):
            first_col = piece_index * hidden_block
            partial_value = jnp.dot(hidden_units[:, first_col:first_col + hidden_block], w_down[layer_index, first_col:first_col + hidden_block], preferred_element_type=jnp.float32)
            feed_sum = feed_sum + lax.optimization_barrier(partial_value.astype(jnp.bfloat16)).astype(jnp.float32)
        stream = (middle.astype(jnp.float32) + feed_sum).astype(jnp.bfloat16)
        new_states.append(jnp.zeros((R, K, H * V), jnp.bfloat16).at[owner].set(chosen))
    hidden_out = jnp.where(valid_rows[:, None], stream, jnp.zeros_like(stream))
    return (hidden_out, jnp.stack(new_states))
```

```python
import math

import jax
import jax.numpy as jnp
from jax import lax
from jax.sharding import PartitionSpec as P

H = 8
K = 256
V = 512
LAYERS = 2


EPSILON = 1e-05
HIGHEST = lax.Precision.HIGHEST


def partner_2(value, axis, stride):
    mask = 2**stride
    pairs = [(source, source ^ mask) for source in range(lax.axis_size(axis))]
    return lax.ppermute(value, axis, pairs)


def to_peers(block, pieces):
    copies = jnp.broadcast_to(block[None], (pieces,) + block.shape)
    return lax.all_to_all(copies, "mlp", split_axis=0, concat_axis=0, tiled=True)


def gather_terms(terms):
    arrived = lax.all_to_all(terms, "mlp", split_axis=0, concat_axis=0, tiled=True)
    return jnp.sum(arrived.astype(jnp.float32), axis=0)


def layer_norm(values, scales):
    widened = values.astype(jnp.float32)
    center = jnp.mean(widened, axis=-1, keepdims=True)
    shifted = widened - center
    spread = jnp.mean(shifted * shifted, axis=-1, keepdims=True)
    return (shifted * lax.rsqrt(spread + EPSILON) * scales).astype(jnp.bfloat16)


def rotate(vectors, positions):
    halfway = vectors.shape[-1] // 2
    frequencies = jnp.exp(jnp.arange(halfway, dtype=jnp.float32) * (-math.log(10000.0) / halfway))
    angles = positions[..., None] * frequencies
    cosine = jnp.cos(angles)
    sine_part = jnp.sin(angles)
    first_half = vectors[..., :halfway]
    second = vectors[..., halfway:]
    return jnp.concatenate(
        [first_half * cosine - second * sine_part, second * cosine + first_half * sine_part],
        axis=-1,
    )


def shards(
    hidden_in,
    draft_len,
    accepted,
    pos_offset,
    owner,
    init_state,
    norm_gain,
    w_query,
    w_key,
    w_value,
    w_gate,
    w_out,
    w_up,
    w_down,
):
    groups = lax.axis_size("req")
    pieces = lax.axis_size("mlp")
    my_group = lax.axis_index("req")
    my_piece = lax.axis_index("mlp")
    tok_rows = hidden_in.shape[0]
    req_rows = draft_len.shape[0]
    slots = tok_rows // req_rows
    block_cols = w_value.shape[2]
    key_rows = K // pieces
    head_span = pieces // H
    split_bits = head_span.bit_length() - 1
    head_index = my_piece // head_span
    decays = 1.0 - jnp.exp2(-5.0 - jnp.arange(H, dtype=jnp.float32))
    log_decay = jnp.log(jnp.sum(jnp.where(jnp.arange(H) == head_index, decays, 0.0)))
    slot_steps = jnp.arange(slots, dtype=jnp.int32)
    step_float = slot_steps.astype(jnp.float32)
    positions = (pos_offset[:, None] + slot_steps[None, :]).reshape(tok_rows).astype(jnp.float32)
    valid_rows = (slot_steps[None, :] < draft_len[:, None]).reshape(tok_rows)
    inter_decay = jnp.exp((step_float + 1.0) * log_decay)
    step_gap = step_float[:, None] - step_float[None, :]
    intra_decay = jnp.where(step_gap >= 0, jnp.exp(jnp.maximum(step_gap, 0.0) * log_decay), 0.0)
    taken_count = accepted.astype(jnp.float32)
    select_gap = taken_count[:, None] - 1.0 - step_float[None, :]
    select_weights = jnp.where(
        select_gap >= 0, jnp.exp(jnp.maximum(select_gap, 0.0) * log_decay), 0.0
    )
    carry_decay = jnp.exp(taken_count * log_decay)
    capacity = 2 * req_rows // groups
    own_slots = lax.dynamic_slice_in_dim(owner, my_group * req_rows, req_rows)
    local_index = jnp.arange(req_rows, dtype=jnp.int32)
    send_group = own_slots // req_rows
    earlier = (send_group[:, None] == send_group[None, :]) & (
        local_index[None, :] < local_index[:, None]
    )
    send_place = jnp.sum(earlier.astype(jnp.int32), axis=1)
    group_ids = jnp.arange(groups, dtype=jnp.int32)
    place_ids = jnp.arange(capacity, dtype=jnp.int32)
    send_table = (
        (send_group[None, None, :] == group_ids[:, None, None])
        & (send_place[None, None, :] == place_ids[None, :, None])
    ).astype(jnp.bfloat16)
    everyone = jnp.arange(owner.shape[0], dtype=jnp.int32)
    all_group = everyone // req_rows
    all_target = owner // req_rows
    peer_mask = (
        (all_group[:, None] == all_group[None, :])
        & (all_target[:, None] == all_target[None, :])
        & (everyone[None, :] < everyone[:, None])
    )
    all_place = jnp.sum(peer_mask.astype(jnp.int32), axis=1)
    matched = (owner[None, :] == my_group * req_rows + local_index[:, None]).astype(jnp.float32)
    group_hot = (all_group[:, None] == group_ids[None, :]).astype(jnp.float32)
    place_hot = (all_place[:, None] == place_ids[None, :]).astype(jnp.float32)
    recv_table = jnp.einsum("tr,rg,rc->tgc", matched, group_hot, place_hot).astype(jnp.bfloat16)
    own_rows = tok_rows // pieces
    full_rows = to_peers(hidden_in, pieces).transpose(1, 0, 2).reshape(tok_rows, -1)
    width = full_rows.shape[1]
    stream = lax.dynamic_slice_in_dim(full_rows, my_piece * own_rows, own_rows)
    home_states = []
    for layer_index in range(LAYERS):
        if layer_index == 0:
            normed = layer_norm(full_rows, norm_gain[layer_index, 0])
        else:
            normed = to_peers(layer_norm(stream, norm_gain[layer_index, 0]), pieces)
            normed = normed.reshape(tok_rows, width)
        query_part = jnp.dot(normed, w_query[layer_index], preferred_element_type=jnp.float32)
        key_part = jnp.dot(normed, w_key[layer_index], preferred_element_type=jnp.float32)
        paired = jnp.stack([query_part, key_part])
        bit_index = 0
        partner = partner_2(paired.astype(jnp.bfloat16), "mlp", bit_index).astype(paired.dtype)
        upper_half = my_piece // (1 << bit_index) % 2
        paired = jnp.where(
            upper_half == 1,
            jnp.concatenate([partner, paired], axis=2),
            jnp.concatenate([paired, partner], axis=2),
        )
        queries = rotate(paired[0], positions)
        keys_now = rotate(paired[1], positions) * K ** (-0.5)
        values_now = jnp.dot(normed, w_value[layer_index], preferred_element_type=jnp.float32)
        gate_values = jnp.dot(normed, w_gate[layer_index], preferred_element_type=jnp.float32)
        query_blocks = queries.reshape(req_rows, slots, K)
        key_blocks = keys_now.reshape(req_rows, slots, K)
        value_blocks = values_now.reshape(req_rows, slots, block_cols)
        memory = init_state[layer_index].astype(jnp.float32)
        carried = (
            jnp.einsum("rtk,rkv->rtv", query_blocks, memory, precision=HIGHEST)
            * inter_decay[None, :, None]
        )
        scores = (
            jnp.einsum("rtk,rsk->rts", query_blocks, key_blocks, precision=HIGHEST)
            * intra_decay[None]
        )
        retained = carried + jnp.einsum("rts,rsv->rtv", scores, value_blocks, precision=HIGHEST)
        weighted = key_blocks * select_weights[:, :, None]
        chosen = (
            carry_decay[:, None, None] * memory
            + jnp.einsum("rsk,rsv->rkv", weighted, value_blocks, precision=HIGHEST)
        ).astype(jnp.bfloat16)
        flattened = retained.reshape(tok_rows, block_cols)
        moments = jnp.stack([jnp.sum(flattened, axis=1), jnp.sum(flattened * flattened, axis=1)])
        bit_index = 0
        moments = moments + partner_2(moments, "mlp", bit_index)
        center = moments[0] / V
        spread = moments[1] / V - center * center
        normalized = (flattened - center[:, None]) * lax.rsqrt(spread + EPSILON)[:, None]
        mixed_in = (normalized * jax.nn.silu(gate_values)).astype(jnp.bfloat16)
        partial_out = jnp.dot(mixed_in, w_out[layer_index], preferred_element_type=jnp.float32)
        shared = gather_terms(partial_out.astype(jnp.bfloat16).reshape(pieces, own_rows, width))
        middle = (stream.astype(jnp.float32) + shared).astype(jnp.bfloat16)
        normed_mid = to_peers(layer_norm(middle, norm_gain[layer_index, 1]), pieces)
        normed_mid = normed_mid.reshape(tok_rows, width)
        hidden_units = jax.nn.gelu(
            jnp.dot(normed_mid, w_up[layer_index], preferred_element_type=jnp.float32),
            approximate=False,
        ).astype(jnp.bfloat16)
        down_terms = jnp.dot(hidden_units, w_down[layer_index], preferred_element_type=jnp.float32)
        if layer_index + 1 < LAYERS:
            feed_sum = gather_terms(
                down_terms.astype(jnp.bfloat16).reshape(pieces, own_rows, width)
            )
            stream = (middle.astype(jnp.float32) + feed_sum).astype(jnp.bfloat16)
        else:
            owned = jnp.arange(pieces)[:, None, None] == my_piece
            with_rows = down_terms.reshape(pieces, own_rows, width) + jnp.where(
                owned, middle.astype(jnp.float32)[None], 0.0
            )
            by_column = with_rows.astype(jnp.bfloat16).reshape(tok_rows, pieces, width // pieces)
            stream = gather_terms(by_column.transpose(1, 0, 2)).astype(jnp.bfloat16)
        sections = chosen.reshape(req_rows, pieces, key_rows, block_cols)
        routed = jnp.einsum(
            "gci,ijkb->gjckb", send_table, sections, preferred_element_type=jnp.float32
        ).astype(jnp.bfloat16)
        arrived = lax.all_to_all(
            routed.reshape(groups * pieces, capacity, key_rows, block_cols),
            ("req", "mlp"),
            split_axis=0,
            concat_axis=0,
            tiled=True,
        ).reshape(groups, pieces, capacity, key_rows, block_cols)
        placed = jnp.einsum(
            "tgc,gjckb->tkjb", recv_table, arrived, preferred_element_type=jnp.float32
        ).astype(jnp.bfloat16)
        home_states.append(placed.reshape(req_rows, key_rows, pieces * block_cols))
    hidden_out = jnp.where(valid_rows[:, None], stream, jnp.zeros_like(stream))
    return (hidden_out, jnp.stack(home_states))


def solution(mesh):
    in_specs = (
        P("req", "mlp"),
        P("req"),
        P("req"),
        P("req"),
        P(),
        P(None, "req", None, "mlp"),
        P(),
        P(None, None, "mlp"),
        P(None, None, "mlp"),
        P(None, None, "mlp"),
        P(None, None, "mlp"),
        P(None, "mlp", None),
        P(None, None, "mlp"),
        P(None, "mlp", None),
    )
    out_specs = (P("req", "mlp"), P(None, "req", "mlp", None))
    return jax.shard_map(shards, mesh=mesh, in_specs=in_specs, out_specs=out_specs, check_vma=False)
```

```python
import math

import jax
import jax.numpy as jnp
from jax import lax
from jax.sharding import PartitionSpec as P

H = 8
K = 256
V = 512
LAYERS = 2


EPSILON = 1e-05
HIGHEST = lax.Precision.HIGHEST


def partner_2(value, axis, stride):
    mask = 2**stride
    pairs = [(source, source ^ mask) for source in range(lax.axis_size(axis))]
    return lax.ppermute(value, axis, pairs)


def swap_groups(value, mask):
    pairs = [(source, source ^ mask) for source in range(lax.axis_size("req"))]
    return lax.ppermute(value, "req", pairs)


def to_peers(block, pieces):
    copies = jnp.broadcast_to(block[None], (pieces,) + block.shape)
    return lax.all_to_all(copies, "mlp", split_axis=0, concat_axis=0, tiled=True)


def gather_terms(terms):
    arrived = lax.all_to_all(terms, "mlp", split_axis=0, concat_axis=0, tiled=True)
    return jnp.sum(arrived.astype(jnp.float32), axis=0)


def layer_norm(values, scales):
    widened = values.astype(jnp.float32)
    center = jnp.mean(widened, axis=-1, keepdims=True)
    shifted = widened - center
    spread = jnp.mean(shifted * shifted, axis=-1, keepdims=True)
    return (shifted * lax.rsqrt(spread + EPSILON) * scales).astype(jnp.bfloat16)


def rotate(vectors, positions):
    halfway = vectors.shape[-1] // 2
    frequencies = jnp.exp(jnp.arange(halfway, dtype=jnp.float32) * (-math.log(10000.0) / halfway))
    angles = positions[..., None] * frequencies
    cosine = jnp.cos(angles)
    sine_part = jnp.sin(angles)
    first_half = vectors[..., :halfway]
    second = vectors[..., halfway:]
    return jnp.concatenate(
        [first_half * cosine - second * sine_part, second * cosine + first_half * sine_part],
        axis=-1,
    )


def shards(
    hidden_in,
    draft_len,
    accepted,
    pos_offset,
    owner,
    init_state,
    norm_gain,
    w_query,
    w_key,
    w_value,
    w_gate,
    w_out,
    w_up,
    w_down,
):
    groups = lax.axis_size("req")
    pieces = lax.axis_size("mlp")
    my_group = lax.axis_index("req")
    my_piece = lax.axis_index("mlp")
    tok_rows = hidden_in.shape[0]
    req_rows = draft_len.shape[0]
    slots = tok_rows // req_rows
    block_cols = w_value.shape[2]
    key_rows = K // pieces
    head_span = pieces // H
    split_bits = head_span.bit_length() - 1
    head_index = my_piece // head_span
    decays = 1.0 - jnp.exp2(-5.0 - jnp.arange(H, dtype=jnp.float32))
    log_decay = jnp.log(jnp.sum(jnp.where(jnp.arange(H) == head_index, decays, 0.0)))
    slot_steps = jnp.arange(slots, dtype=jnp.int32)
    step_float = slot_steps.astype(jnp.float32)
    positions = (pos_offset[:, None] + slot_steps[None, :]).reshape(tok_rows).astype(jnp.float32)
    valid_rows = (slot_steps[None, :] < draft_len[:, None]).reshape(tok_rows)
    inter_decay = jnp.exp((step_float + 1.0) * log_decay)
    step_gap = step_float[:, None] - step_float[None, :]
    intra_decay = jnp.where(step_gap >= 0, jnp.exp(jnp.maximum(step_gap, 0.0) * log_decay), 0.0)
    taken_count = accepted.astype(jnp.float32)
    select_gap = taken_count[:, None] - 1.0 - step_float[None, :]
    select_weights = jnp.where(
        select_gap >= 0, jnp.exp(jnp.maximum(select_gap, 0.0) * log_decay), 0.0
    )
    carry_decay = jnp.exp(taken_count * log_decay)
    capacity = 2 * req_rows // groups
    own_slots = lax.dynamic_slice_in_dim(owner, my_group * req_rows, req_rows)
    local_index = jnp.arange(req_rows, dtype=jnp.int32)
    send_group = own_slots // req_rows
    earlier = (send_group[:, None] == send_group[None, :]) & (
        local_index[None, :] < local_index[:, None]
    )
    send_place = jnp.sum(earlier.astype(jnp.int32), axis=1)
    group_ids = jnp.arange(groups, dtype=jnp.int32)
    place_ids = jnp.arange(capacity, dtype=jnp.int32)
    step_groups = my_group ^ group_ids
    send_table = (
        (send_group[None, None, :] == step_groups[:, None, None])
        & (send_place[None, None, :] == place_ids[None, :, None])
    ).astype(jnp.bfloat16)
    everyone = jnp.arange(owner.shape[0], dtype=jnp.int32)
    all_group = everyone // req_rows
    all_target = owner // req_rows
    peer_mask = (
        (all_group[:, None] == all_group[None, :])
        & (all_target[:, None] == all_target[None, :])
        & (everyone[None, :] < everyone[:, None])
    )
    all_place = jnp.sum(peer_mask.astype(jnp.int32), axis=1)
    matched = (owner[None, :] == my_group * req_rows + local_index[:, None]).astype(jnp.float32)
    group_hot = (all_group[:, None] == step_groups[None, :]).astype(jnp.float32)
    place_hot = (all_place[:, None] == place_ids[None, :]).astype(jnp.float32)
    recv_table = jnp.einsum("tr,rg,rc->tgc", matched, group_hot, place_hot).astype(jnp.bfloat16)
    own_rows = tok_rows // pieces
    full_rows = to_peers(hidden_in, pieces).transpose(1, 0, 2).reshape(tok_rows, -1)
    width = full_rows.shape[1]
    stream = lax.dynamic_slice_in_dim(full_rows, my_piece * own_rows, own_rows)
    home_states = []
    for layer_index in range(LAYERS):
        if layer_index == 0:
            normed = layer_norm(full_rows, norm_gain[layer_index, 0])
        else:
            normed = to_peers(layer_norm(stream, norm_gain[layer_index, 0]), pieces)
            normed = normed.reshape(tok_rows, width)
        query_part = jnp.dot(normed, w_query[layer_index], preferred_element_type=jnp.float32)
        key_part = jnp.dot(normed, w_key[layer_index], preferred_element_type=jnp.float32)
        paired = jnp.stack([query_part, key_part])
        bit_index = 0
        partner = partner_2(paired.astype(jnp.bfloat16), "mlp", bit_index).astype(paired.dtype)
        upper_half = my_piece // (1 << bit_index) % 2
        paired = jnp.where(
            upper_half == 1,
            jnp.concatenate([partner, paired], axis=2),
            jnp.concatenate([paired, partner], axis=2),
        )
        queries = rotate(paired[0], positions)
        keys_now = rotate(paired[1], positions) * K ** (-0.5)
        values_now = jnp.dot(normed, w_value[layer_index], preferred_element_type=jnp.float32)
        gate_values = jnp.dot(normed, w_gate[layer_index], preferred_element_type=jnp.float32)
        query_blocks = queries.reshape(req_rows, slots, K)
        key_blocks = keys_now.reshape(req_rows, slots, K)
        value_blocks = values_now.reshape(req_rows, slots, block_cols)
        memory = init_state[layer_index].astype(jnp.float32)
        carried = (
            jnp.einsum("rtk,rkv->rtv", query_blocks, memory, precision=HIGHEST)
            * inter_decay[None, :, None]
        )
        scores = (
            jnp.einsum("rtk,rsk->rts", query_blocks, key_blocks, precision=HIGHEST)
            * intra_decay[None]
        )
        retained = carried + jnp.einsum("rts,rsv->rtv", scores, value_blocks, precision=HIGHEST)
        weighted = key_blocks * select_weights[:, :, None]
        chosen = (
            carry_decay[:, None, None] * memory
            + jnp.einsum("rsk,rsv->rkv", weighted, value_blocks, precision=HIGHEST)
        ).astype(jnp.bfloat16)
        flattened = retained.reshape(tok_rows, block_cols)
        moments = jnp.stack([jnp.sum(flattened, axis=1), jnp.sum(flattened * flattened, axis=1)])
        bit_index = 0
        moments = moments + partner_2(moments, "mlp", bit_index)
        center = moments[0] / V
        spread = moments[1] / V - center * center
        normalized = (flattened - center[:, None]) * lax.rsqrt(spread + EPSILON)[:, None]
        mixed_in = (normalized * jax.nn.silu(gate_values)).astype(jnp.bfloat16)
        partial_out = jnp.dot(mixed_in, w_out[layer_index], preferred_element_type=jnp.float32)
        shared = gather_terms(partial_out.astype(jnp.bfloat16).reshape(pieces, own_rows, width))
        middle = (stream.astype(jnp.float32) + shared).astype(jnp.bfloat16)
        normed_mid = layer_norm(middle, norm_gain[layer_index, 1])
        by_key = chosen.transpose(1, 0, 2).reshape(pieces, key_rows, req_rows * block_cols)
        mixed = jnp.concatenate(
            [jnp.broadcast_to(normed_mid[None], (pieces, own_rows, width)), by_key], axis=1
        )
        landed = lax.all_to_all(mixed, "mlp", split_axis=0, concat_axis=0, tiled=True)
        normed_mid = landed[:, :own_rows].reshape(tok_rows, width)
        sections = landed[:, own_rows:].reshape(pieces, key_rows, req_rows, block_cols)
        routed = jnp.einsum(
            "gcr,ikrb->gckib", send_table, sections, preferred_element_type=jnp.float32
        ).astype(jnp.bfloat16)
        arrived = jnp.stack([routed[0]] + [swap_groups(routed[k], k) for k in range(1, groups)])
        placed = jnp.einsum(
            "tgc,gckib->tkib", recv_table, arrived, preferred_element_type=jnp.float32
        ).astype(jnp.bfloat16)
        home_states.append(placed.reshape(req_rows, key_rows, pieces * block_cols))
        hidden_units = jax.nn.gelu(
            jnp.dot(normed_mid, w_up[layer_index], preferred_element_type=jnp.float32),
            approximate=False,
        ).astype(jnp.bfloat16)
        down_terms = jnp.dot(hidden_units, w_down[layer_index], preferred_element_type=jnp.float32)
        if layer_index + 1 < LAYERS:
            feed_sum = gather_terms(
                down_terms.astype(jnp.bfloat16).reshape(pieces, own_rows, width)
            )
            stream = (middle.astype(jnp.float32) + feed_sum).astype(jnp.bfloat16)
        else:
            owned = jnp.arange(pieces)[:, None, None] == my_piece
            with_rows = down_terms.reshape(pieces, own_rows, width) + jnp.where(
                owned, middle.astype(jnp.float32)[None], 0.0
            )
            by_column = with_rows.astype(jnp.bfloat16).reshape(tok_rows, pieces, width // pieces)
            stream = gather_terms(by_column.transpose(1, 0, 2)).astype(jnp.bfloat16)
    hidden_out = jnp.where(valid_rows[:, None], stream, jnp.zeros_like(stream))
    return (hidden_out, jnp.stack(home_states))


def solution(mesh):
    in_specs = (
        P("req", "mlp"),
        P("req"),
        P("req"),
        P("req"),
        P(),
        P(None, "req", None, "mlp"),
        P(),
        P(None, None, "mlp"),
        P(None, None, "mlp"),
        P(None, None, "mlp"),
        P(None, None, "mlp"),
        P(None, "mlp", None),
        P(None, None, "mlp"),
        P(None, "mlp", None),
    )
    out_specs = (P("req", "mlp"), P(None, "req", "mlp", None))
    return jax.shard_map(shards, mesh=mesh, in_specs=in_specs, out_specs=out_specs, check_vma=False)
```

```python
import functools
import math

import jax
import jax.numpy as jnp
from jax import lax
from jax.experimental import pallas as pl
from jax.experimental.pallas import tpu as pltpu
from jax.sharding import PartitionSpec as P

H = 8
K = 256
V = 512
LAYERS = 2

EPSILON = 1e-05
F32 = jnp.float32
BF16 = jnp.bfloat16
VMEM_BYTES = 24 * 1024 * 1024


def swap(value, axis, mask):
    pairs = [(source, source ^ mask) for source in range(lax.axis_size(axis))]
    return lax.ppermute(value, axis, pairs)


def exchange(blocks):
    return lax.all_to_all(blocks, "mlp", split_axis=0, concat_axis=0, tiled=True)


def layer_norm(values, scales):
    widened = values.astype(F32)
    center = jnp.mean(widened, axis=-1, keepdims=True)
    shifted = widened - center
    variance = jnp.mean(shifted * shifted, axis=-1, keepdims=True)
    return (shifted * lax.rsqrt(variance + EPSILON) * scales).astype(BF16)


def any_spec():
    return pl.BlockSpec(memory_space=pl.ANY)


def smem_spec():
    return pl.BlockSpec(memory_space=pltpu.SMEM)


def whole(shape):
    return pl.BlockSpec(shape, lambda i: (0,) * len(shape))


def layer_block(shape, layer):
    return pl.BlockSpec((1,) + shape, lambda i: (layer,) + (0,) * len(shape))


def params():
    return pltpu.CompilerParams(vmem_limit_bytes=VMEM_BYTES)


def cost(flops, nbytes):
    return pl.CostEstimate(flops=flops, bytes_accessed=nbytes, transcendentals=0)


def retention_body(
    half_ref, carry_ref, own_ref, other_ref, table_ref, select_ref, value_ref, state_ref,
    retained_ref, moment_ref, chosen_ref,
):
    upper = half_ref[0] == 1
    requests = select_ref.shape[0]
    rows = value_ref.shape[0]
    slots = rows // requests
    cols = value_ref.shape[1]
    own_q, own_k = own_ref[0].astype(F32), own_ref[1].astype(F32)
    other_q, other_k = other_ref[0].astype(F32), other_ref[1].astype(F32)
    q_low, q_high = jnp.where(upper, other_q, own_q), jnp.where(upper, own_q, other_q)
    k_low, k_high = jnp.where(upper, other_k, own_k), jnp.where(upper, own_k, other_k)
    q_cos, q_sin, k_cos, k_sin = table_ref[0], table_ref[1], table_ref[2], table_ref[3]
    queries = jnp.concatenate(
        [q_low * q_cos - q_high * q_sin, q_high * q_cos + q_low * q_sin], axis=1
    ).astype(BF16)
    keys = jnp.concatenate(
        [k_low * k_cos - k_high * k_sin, k_high * k_cos + k_low * k_sin], axis=1
    )
    values = value_ref[...]
    scores = lax.dot_general(
        queries, keys.astype(BF16), (((1,), (1,)), ((), ())), preferred_element_type=F32
    )
    scores = (scores * table_ref[4]).astype(BF16)
    inner = jnp.dot(scores, values, preferred_element_type=F32)
    parts = []
    for r in range(requests):
        low, high = r * slots, (r + 1) * slots
        parts.append(
            inner[low:high]
            + jnp.dot(queries[low:high], state_ref[0, r], preferred_element_type=F32)
        )
    retained = jnp.concatenate(parts, axis=0)
    retained_ref[...] = retained
    lane = lax.broadcasted_iota(jnp.int32, (rows, 128), 1)
    total = jnp.sum(retained, axis=1, keepdims=True)
    squares = jnp.sum(retained * retained, axis=1, keepdims=True)
    columns = jnp.where(lane == 0, total, jnp.where(lane == 1, squares, 0.0))
    moment_ref[...] = jnp.transpose(columns)[:8]
    flipped = jnp.transpose(keys)
    for r in range(requests):
        weighted = (flipped * select_ref[r : r + 1, :]).astype(BF16)
        update = jnp.dot(weighted, values, preferred_element_type=F32)
        kept = carry_ref[r] * state_ref[0, r].astype(F32)
        chosen_ref[:, r * cols : (r + 1) * cols] = (kept + update).astype(BF16)


def retention(layer, half, carry, own, other, tables, select, values, states):
    rows, cols = values.shape
    requests, key_size = states.shape[1], states.shape[2]
    return pl.pallas_call(
        retention_body,
        grid=(1,),
        in_specs=[
            smem_spec(), smem_spec(), whole(own.shape), whole(other.shape),
            whole(tables.shape), whole(select.shape), whole(values.shape),
            layer_block(states.shape[1:], layer),
        ],
        out_specs=[
            whole((rows, cols)), whole((8, rows)), whole((key_size, requests * cols)),
        ],
        out_shape=[
            jax.ShapeDtypeStruct((rows, cols), F32),
            jax.ShapeDtypeStruct((8, rows), F32),
            jax.ShapeDtypeStruct((key_size, requests * cols), BF16),
        ],
        compiler_params=params(),
        cost_estimate=cost(4 * rows * key_size * cols * requests, 4 * 1024 * 1024),
        name="retention",
    )(half, carry, own, other, tables, select, values, states)


def project_body(
    retained_ref, gate_ref, mine_ref, theirs_ref, weight_ref, chosen_ref, out_ref,
    rows_ref, state_sem, rows_sem,
):
    pieces, own_rows, width = rows_ref.shape
    state_copy = pltpu.make_async_copy(
        chosen_ref, out_ref.at[:, pl.ds(own_rows, chosen_ref.shape[1])], state_sem
    )
    state_copy.start()
    rows = retained_ref.shape[0]
    sums = mine_ref[...] + theirs_ref[...]
    padded = jnp.concatenate([sums, jnp.zeros((128 - 8, rows), F32)], axis=0)
    columns = jnp.transpose(padded)
    center = columns[:, 0:1] / V
    variance = columns[:, 1:2] / V - center * center
    gate = gate_ref[...]
    mixed = (retained_ref[...] - center) * lax.rsqrt(variance + EPSILON)
    mixed = (mixed * (gate / (1.0 + jnp.exp(-gate)))).astype(BF16)
    result = jnp.dot(mixed, weight_ref[0], preferred_element_type=F32)
    for i in range(pieces):
        rows_ref[i] = result[i * own_rows : (i + 1) * own_rows].astype(BF16)
    rows_copy = pltpu.make_async_copy(rows_ref, out_ref.at[:, pl.ds(0, own_rows)], rows_sem)
    rows_copy.start()
    state_copy.wait()
    rows_copy.wait()


def project(layer, pieces, retained, gate, mine, theirs, weights, chosen):
    rows, cols = retained.shape
    width = weights.shape[2]
    own_rows = rows // pieces
    key_rows = chosen.shape[1]
    return pl.pallas_call(
        project_body,
        grid=(1,),
        in_specs=[
            whole((rows, cols)), whole((rows, cols)), whole(mine.shape), whole(theirs.shape),
            layer_block(weights.shape[1:], layer), any_spec(),
        ],
        out_specs=any_spec(),
        out_shape=jax.ShapeDtypeStruct((pieces, own_rows + key_rows, width), BF16),
        scratch_shapes=[
            pltpu.VMEM((pieces, own_rows, width), BF16),
            pltpu.SemaphoreType.DMA(()),
            pltpu.SemaphoreType.DMA(()),
        ],
        compiler_params=params(),
        cost_estimate=cost(2 * rows * cols * width, 4 * 1024 * 1024),
        name="project",
    )(retained, gate, mine, theirs, weights, chosen)


def settle_body(term_ref, base_ref, gain_ref, sum_ref, out_ref, held_ref, sem):
    pieces, own_rows, width = held_ref.shape
    fetch = pltpu.make_async_copy(term_ref.at[:, pl.ds(0, own_rows)], held_ref, sem)
    fetch.start()
    fetch.wait()
    total = jnp.zeros((own_rows, width), F32)
    for i in range(pieces):
        total = total + held_ref[i].astype(F32)
    rounded = (base_ref[...].astype(F32) + total).astype(BF16)
    sum_ref[...] = rounded
    widened = rounded.astype(F32)
    shifted = widened - jnp.mean(widened, axis=-1, keepdims=True)
    variance = jnp.mean(shifted * shifted, axis=-1, keepdims=True)
    normed = (shifted * lax.rsqrt(variance + EPSILON) * gain_ref[...]).astype(BF16)
    for i in range(pieces):
        out_ref[i] = normed


def settle(terms, base, gain):
    pieces, width = terms.shape[0], terms.shape[2]
    own_rows = base.shape[0]
    block = (pieces, own_rows, width)
    return pl.pallas_call(
        settle_body,
        grid=(1,),
        in_specs=[any_spec(), whole(base.shape), whole((1, width))],
        out_specs=[whole(base.shape), whole(block)],
        out_shape=[
            jax.ShapeDtypeStruct(base.shape, BF16),
            jax.ShapeDtypeStruct(block, BF16),
        ],
        scratch_shapes=[pltpu.VMEM(block, BF16), pltpu.SemaphoreType.DMA(())],
        compiler_params=params(),
        cost_estimate=cost(4 * pieces * own_rows * width, 1024 * 1024),
        name="settle",
    )(terms, base, gain.reshape(1, width))


def pack_body(own_rows, cols, pick_ref, landed_ref, *refs):
    outs, held_ref, sem = refs[:-2], refs[-2], refs[-1]
    pieces, key_rows = held_ref.shape[0], held_ref.shape[1]
    fetch = pltpu.make_async_copy(
        landed_ref.at[:, pl.ds(own_rows, key_rows)], held_ref, sem
    )
    fetch.start()
    fetch.wait()
    for g, out_ref in enumerate(outs):
        for c in range(out_ref.shape[0]):
            start = pl.multiple_of(pick_ref[g * out_ref.shape[0] + c] * cols, cols)
            for i in range(pieces):
                out_ref[c, :, i * cols : (i + 1) * cols] = held_ref[i, :, pl.ds(start, cols)]


def pack(picks, landed, groups, own_rows, cols):
    pieces, key_rows, width = landed.shape[0], landed.shape[1] - own_rows, landed.shape[2]
    capacity = picks.shape[0] // groups
    block = (capacity, key_rows, pieces * cols)
    return pl.pallas_call(
        functools.partial(pack_body, own_rows, cols),
        grid=(1,),
        in_specs=[smem_spec(), any_spec()],
        out_specs=[whole(block)] * groups,
        out_shape=[jax.ShapeDtypeStruct(block, BF16)] * groups,
        scratch_shapes=[
            pltpu.VMEM((pieces, key_rows, width), BF16),
            pltpu.SemaphoreType.DMA(()),
        ],
        compiler_params=params(),
        cost_estimate=cost(1024, 3 * 1024 * 1024),
        name="pack",
    )(picks, landed)


def place_body(layer, groups, slot_ref, *refs):
    blocks = refs[:groups]
    out_ref, sems = refs[-2], refs[-1]
    capacity = blocks[0].shape[0]
    for start in (True, False):
        for g in range(groups):
            for c in range(capacity):
                n = g * capacity + c
                slot = slot_ref[n]

                @pl.when(slot >= 0)
                def _():
                    copy = pltpu.make_async_copy(
                        blocks[g].at[c], out_ref.at[layer, jnp.maximum(slot, 0)], sems.at[n]
                    )
                    if start:
                        copy.start()
                    else:
                        copy.wait()


def place(layer, slots, blocks, shape, previous):
    groups = len(blocks)
    operands = [slots, *blocks] + ([] if previous is None else [previous])
    aliases = {} if previous is None else {groups + 1: 0}
    return pl.pallas_call(
        functools.partial(place_body, layer, groups),
        grid=(1,),
        in_specs=[smem_spec()] + [any_spec()] * (len(operands) - 1),
        out_specs=any_spec(),
        out_shape=jax.ShapeDtypeStruct(shape, BF16),
        scratch_shapes=[pltpu.SemaphoreType.DMA((slots.shape[0],))],
        input_output_aliases=aliases,
        compiler_params=params(),
        cost_estimate=cost(1024, 2 * 1024 * 1024),
        name="place",
    )(*operands)


def shards(
    hidden_in,
    draft_len,
    accepted,
    pos_offset,
    owner,
    init_state,
    norm_gain,
    w_query,
    w_key,
    w_value,
    w_gate,
    w_out,
    w_up,
    w_down,
):
    groups = lax.axis_size("req")
    pieces = lax.axis_size("mlp")
    my_group = lax.axis_index("req")
    my_piece = lax.axis_index("mlp")
    tok_rows = hidden_in.shape[0]
    width = hidden_in.shape[1] * pieces
    req_rows = draft_len.shape[0]
    slots = tok_rows // req_rows
    own_rows = tok_rows // pieces
    block_cols = w_value.shape[2]
    key_rows = K // pieces
    head_span = pieces // H
    head_index = my_piece // head_span
    upper_half = (my_piece % head_span).astype(jnp.int32).reshape(1)
    decays = 1.0 - jnp.exp2(-5.0 - jnp.arange(H, dtype=F32))
    log_decay = jnp.log(jnp.sum(jnp.where(jnp.arange(H) == head_index, decays, 0.0)))

    token = jnp.arange(tok_rows, dtype=jnp.int32)
    step = (token % slots).astype(F32)
    first = token // slots
    slot_steps = jnp.arange(slots, dtype=jnp.int32)
    positions = (pos_offset[:, None] + slot_steps[None, :]).reshape(tok_rows).astype(F32)
    valid_rows = (slot_steps[None, :] < draft_len[:, None]).reshape(tok_rows)
    halfway = K // 2
    frequencies = jnp.exp(jnp.arange(halfway, dtype=F32) * (-math.log(10000.0) / halfway))
    angles = positions[:, None] * frequencies[None, :]
    cosine, sine = jnp.cos(angles), jnp.sin(angles)
    grown = jnp.exp((step + 1.0) * log_decay)[:, None]
    shrink = jnp.exp(-(step + 1.0) * log_decay)[None, :]
    inside = (first[:, None] == first[None, :]) & (step[:, None] >= step[None, :])
    tables = jnp.stack(
        [
            cosine * grown,
            sine * grown,
            cosine * K ** (-0.5),
            sine * K ** (-0.5),
            jnp.where(inside, shrink, 0.0),
        ]
    )
    taken_count = accepted.astype(F32)
    gap = taken_count[:, None] - 1.0 - step[None, :]
    picked = (first[None, :] == jnp.arange(req_rows)[:, None]) & (gap >= 0)
    select = jnp.where(picked, jnp.exp(jnp.maximum(gap, 0.0) * log_decay), 0.0)
    carry_decay = jnp.exp(taken_count * log_decay)

    capacity = 2 * req_rows // groups
    everyone = jnp.arange(owner.shape[0], dtype=jnp.int32)
    all_group = everyone // req_rows
    all_target = owner // req_rows
    peer_mask = (
        (all_group[:, None] == all_group[None, :])
        & (all_target[:, None] == all_target[None, :])
        & (everyone[None, :] < everyone[:, None])
    )
    all_place = jnp.sum(peer_mask.astype(jnp.int32), axis=1)
    step_groups = my_group ^ jnp.arange(groups, dtype=jnp.int32)
    place_ids = jnp.arange(capacity, dtype=jnp.int32)
    at_place = all_place[None, None, :] == place_ids[None, :, None]
    goes = (
        (all_group == my_group)[None, None, :]
        & (all_target[None, None, :] == step_groups[:, None, None])
        & at_place
    )
    picks = jnp.sum(jnp.where(goes, everyone % req_rows, 0), axis=2).reshape(-1)
    comes = (
        (all_target == my_group)[None, None, :]
        & (all_group[None, None, :] == step_groups[:, None, None])
        & at_place
    )
    fills = jnp.sum(jnp.where(comes, owner % req_rows + 1, 0), axis=2).reshape(-1) - 1

    copies = jnp.broadcast_to(hidden_in[None], (pieces,) + hidden_in.shape)
    full_rows = exchange(copies).transpose(1, 0, 2).reshape(tok_rows, width)
    stream = lax.dynamic_slice_in_dim(full_rows, my_piece * own_rows, own_rows)
    normed = layer_norm(full_rows, norm_gain[0, 0])
    home_shape = (LAYERS, req_rows, key_rows, pieces * block_cols)
    home = None
    for layer in range(LAYERS):
        query_part = jnp.dot(normed, w_query[layer], preferred_element_type=F32)
        key_part = jnp.dot(normed, w_key[layer], preferred_element_type=F32)
        own = jnp.stack([query_part, key_part]).astype(BF16)
        other = swap(own, "mlp", 1)
        values = jnp.dot(normed, w_value[layer], preferred_element_type=F32).astype(BF16)
        gate_values = jnp.dot(normed, w_gate[layer], preferred_element_type=F32)
        retained, moments, chosen = retention(
            layer, upper_half, carry_decay, own, other, tables, select, values, init_state
        )
        theirs = swap(moments, "mlp", 1)
        mixed = project(
            layer, pieces, retained, gate_values, moments, theirs, w_out,
            chosen.reshape(pieces, key_rows, req_rows * block_cols),
        )
        if home is not None:
            mixed, home = lax.optimization_barrier((mixed, home))
        landed = exchange(mixed)
        middle, spread_mid = settle(landed, stream, norm_gain[layer, 1])
        outgoing = pack(picks, landed, groups, own_rows, block_cols)
        incoming = [outgoing[0]] + [
            swap(outgoing[mask], "req", mask) for mask in range(1, groups)
        ]
        home = place(layer, fills, incoming, home_shape, home)
        normed_mid = exchange(spread_mid).reshape(tok_rows, width)
        hidden_units = jax.nn.gelu(
            jnp.dot(normed_mid, w_up[layer], preferred_element_type=F32), approximate=False
        ).astype(BF16)
        down_terms = jnp.dot(hidden_units, w_down[layer], preferred_element_type=F32)
        if layer + 1 < LAYERS:
            terms = down_terms.astype(BF16).reshape(pieces, own_rows, width)
            stream, spread_rows = settle(exchange(terms), middle, norm_gain[layer + 1, 0])
            normed = exchange(spread_rows).reshape(tok_rows, width)
        else:
            owned = jnp.arange(pieces)[:, None, None] == my_piece
            with_rows = down_terms.reshape(pieces, own_rows, width) + jnp.where(
                owned, middle.astype(F32)[None], 0.0
            )
            by_column = with_rows.astype(BF16).reshape(tok_rows, pieces, width // pieces)
            arrived = exchange(by_column.transpose(1, 0, 2))
            stream = jnp.sum(arrived.astype(F32), axis=0).astype(BF16)
    hidden_out = jnp.where(valid_rows[:, None], stream, jnp.zeros_like(stream))
    return (hidden_out, home)


def solution(mesh):
    in_specs = (
        P("req", "mlp"),
        P("req"),
        P("req"),
        P("req"),
        P(),
        P(None, "req", None, "mlp"),
        P(),
        P(None, None, "mlp"),
        P(None, None, "mlp"),
        P(None, None, "mlp"),
        P(None, None, "mlp"),
        P(None, "mlp", None),
        P(None, None, "mlp"),
        P(None, "mlp", None),
    )
    out_specs = (P("req", "mlp"), P(None, "req", "mlp", None))
    return jax.shard_map(shards, mesh=mesh, in_specs=in_specs, out_specs=out_specs, check_vma=False)
```

```python
import functools
import math

import jax
import jax.numpy as jnp
from jax import lax
from jax.experimental import pallas as pl
from jax.experimental.pallas import tpu as pltpu
from jax.sharding import PartitionSpec as P

H = 8
K = 256
V = 512
LAYERS = 2

EPSILON = 1e-05
F32 = jnp.float32
BF16 = jnp.bfloat16
VMEM_BYTES = 24 * 1024 * 1024


def swap(value, axis, mask):
    pairs = [(source, source ^ mask) for source in range(lax.axis_size(axis))]
    return lax.ppermute(value, axis, pairs)


def send(blocks):
    return {mask: swap(block, "req", mask) for mask, block in enumerate(blocks, 1)}


def in_order(blocks):
    return [blocks[mask] for mask in sorted(blocks)]


def after(value, blocks, masks):
    tied = lax.optimization_barrier((value, *[blocks[n] for n in masks]))
    return tied[0], {**blocks, **dict(zip(masks, tied[1:]))}


def exchange(blocks):
    return lax.all_to_all(blocks, "mlp", split_axis=0, concat_axis=0, tiled=True)


def layer_norm(values, scales):
    widened = values.astype(F32)
    center = jnp.mean(widened, axis=-1, keepdims=True)
    shifted = widened - center
    variance = jnp.mean(shifted * shifted, axis=-1, keepdims=True)
    return (shifted * lax.rsqrt(variance + EPSILON) * scales).astype(BF16)


def any_spec():
    return pl.BlockSpec(memory_space=pl.ANY)


def in_hbm(block):
    return pltpu.with_memory_space_constraint(block, pltpu.MemorySpace.HBM)


def hbm_spec():
    return pl.BlockSpec(memory_space=pltpu.MemorySpace.HBM)


def smem_spec():
    return pl.BlockSpec(memory_space=pltpu.SMEM)


def whole(shape):
    return pl.BlockSpec(shape, lambda i: (0,) * len(shape))


def layer_block(shape, layer):
    return pl.BlockSpec((1,) + shape, lambda i: (layer,) + (0,) * len(shape))


def params():
    return pltpu.CompilerParams(vmem_limit_bytes=VMEM_BYTES)


def cost(flops, nbytes):
    return pl.CostEstimate(flops=flops, bytes_accessed=nbytes, transcendentals=0)


def retention_body(
    half_ref, own_ref, other_ref, table_ref, weight_ref, value_ref, state_ref,
    retained_ref, moment_ref, factor_ref,
):
    upper = half_ref[0] == 1
    requests = state_ref.shape[1]
    rows = value_ref.shape[0]
    slots = rows // requests
    own_q, own_k = own_ref[0].astype(F32), own_ref[1].astype(F32)
    other_q, other_k = other_ref[0].astype(F32), other_ref[1].astype(F32)
    q_low, q_high = jnp.where(upper, other_q, own_q), jnp.where(upper, own_q, other_q)
    k_low, k_high = jnp.where(upper, other_k, own_k), jnp.where(upper, own_k, other_k)
    q_cos, q_sin, k_cos, k_sin = table_ref[0], table_ref[1], table_ref[2], table_ref[3]
    queries = jnp.concatenate(
        [q_low * q_cos - q_high * q_sin, q_high * q_cos + q_low * q_sin], axis=1
    ).astype(BF16)
    keys = jnp.concatenate(
        [k_low * k_cos - k_high * k_sin, k_high * k_cos + k_low * k_sin], axis=1
    )
    values = value_ref[...]
    scores = lax.dot_general(
        queries, keys.astype(BF16), (((1,), (1,)), ((), ())), preferred_element_type=F32
    )
    scores = (scores * table_ref[4]).astype(BF16)
    inner = jnp.dot(scores, values, preferred_element_type=F32)
    parts = []
    for r in range(requests):
        low, high = r * slots, (r + 1) * slots
        parts.append(
            inner[low:high]
            + jnp.dot(queries[low:high], state_ref[0, r], preferred_element_type=F32)
        )
    retained = jnp.concatenate(parts, axis=0)
    retained_ref[...] = retained
    lane = lax.broadcasted_iota(jnp.int32, (rows, 128), 1)
    total = jnp.sum(retained, axis=1, keepdims=True)
    squares = jnp.sum(retained * retained, axis=1, keepdims=True)
    columns = jnp.where(lane == 0, total, jnp.where(lane == 1, squares, 0.0))
    moment_ref[...] = jnp.transpose(columns)[:8]
    weighted = (keys * weight_ref[:, 0:1]).astype(BF16)
    kept = weight_ref[:, 1:2]
    rough = kept.astype(BF16)
    rest = (kept - rough.astype(F32)).astype(BF16)
    first = lax.broadcasted_iota(jnp.int32, (rows, 1), 0) % slots == 0
    kept = jnp.where(first, rough.astype(F32), rest.astype(F32))
    kept = jnp.broadcast_to(kept, keys.shape).astype(BF16)
    for r in range(requests):
        low, high = r * slots, (r + 1) * slots
        for n, part in enumerate((weighted, values, kept)):
            factor_ref[r, n * slots : (n + 1) * slots] = part[low:high]


def retention(layer, half, own, other, tables, weights, values, states):
    rows, cols = values.shape
    requests, key_size = states.shape[1], states.shape[2]
    factors = (requests, 3 * rows // requests, key_size)
    return pl.pallas_call(
        retention_body,
        grid=(1,),
        in_specs=[
            smem_spec(), whole(own.shape), whole(other.shape), whole(tables.shape),
            whole(weights.shape), whole(values.shape), layer_block(states.shape[1:], layer),
        ],
        out_specs=[whole((rows, cols)), whole((8, rows)), whole(factors)],
        out_shape=[
            jax.ShapeDtypeStruct((rows, cols), F32),
            jax.ShapeDtypeStruct((8, rows), F32),
            jax.ShapeDtypeStruct(factors, BF16),
        ],
        compiler_params=params(),
        cost_estimate=cost(4 * rows * key_size * cols, 2 * 1024 * 1024),
        name="retention",
    )(half, own, other, tables, weights, values, states)


def project_body(retained_ref, gate_ref, mine_ref, theirs_ref, weight_ref, out_ref):
    pieces, own_rows, width = out_ref.shape
    rows = retained_ref.shape[0]
    sums = mine_ref[...] + theirs_ref[...]
    padded = jnp.concatenate([sums, jnp.zeros((128 - 8, rows), F32)], axis=0)
    columns = jnp.transpose(padded)
    center = columns[:, 0:1] / V
    variance = columns[:, 1:2] / V - center * center
    gate = gate_ref[...]
    mixed = (retained_ref[...] - center) * lax.rsqrt(variance + EPSILON)
    mixed = (mixed * (gate / (1.0 + jnp.exp(-gate)))).astype(BF16)
    result = jnp.dot(mixed, weight_ref[0], preferred_element_type=F32)
    for i in range(pieces):
        out_ref[i] = result[i * own_rows : (i + 1) * own_rows].astype(BF16)


def project(layer, pieces, retained, gate, mine, theirs, weights):
    rows, cols = retained.shape
    width = weights.shape[2]
    block = (pieces, rows // pieces, width)
    return pl.pallas_call(
        project_body,
        grid=(1,),
        in_specs=[
            whole((rows, cols)), whole((rows, cols)), whole(mine.shape), whole(theirs.shape),
            layer_block(weights.shape[1:], layer),
        ],
        out_specs=whole(block),
        out_shape=jax.ShapeDtypeStruct(block, BF16),
        compiler_params=params(),
        cost_estimate=cost(2 * rows * cols * width, 2 * 1024 * 1024),
        name="project",
    )(retained, gate, mine, theirs, weights)


def settle_body(term_ref, base_ref, gain_ref, sum_ref, out_ref):
    pieces, own_rows, width = term_ref.shape
    total = jnp.zeros((own_rows, width), F32)
    for i in range(pieces):
        total = total + term_ref[i].astype(F32)
    rounded = (base_ref[...].astype(F32) + total).astype(BF16)
    sum_ref[...] = rounded
    widened = rounded.astype(F32)
    shifted = widened - jnp.mean(widened, axis=-1, keepdims=True)
    variance = jnp.mean(shifted * shifted, axis=-1, keepdims=True)
    normed = (shifted * lax.rsqrt(variance + EPSILON) * gain_ref[...]).astype(BF16)
    for i in range(pieces):
        out_ref[i] = normed


def settle(terms, base, gain):
    width = terms.shape[2]
    return pl.pallas_call(
        settle_body,
        grid=(1,),
        in_specs=[whole(terms.shape), whole(base.shape), whole((1, width))],
        out_specs=[whole(base.shape), whole(terms.shape)],
        out_shape=[
            jax.ShapeDtypeStruct(base.shape, BF16),
            jax.ShapeDtypeStruct(terms.shape, BF16),
        ],
        compiler_params=params(),
        cost_estimate=cost(4 * terms.size, 1024 * 1024),
        name="settle",
    )(terms, base, gain.reshape(1, width))


def pack_body(layers, pick_ref, block_ref, *refs):
    outs, held_ref, in_sems, out_sems = refs[:-3], refs[-3], refs[-2], refs[-1]
    capacity = outs[0].shape[1 if layers else 0]
    for stage in range(3):
        for g, out_ref in enumerate(outs):
            for c in range(capacity):
                n = (g + 1) * capacity + c
                request = pick_ref[n]

                @pl.when(request >= 0)
                def _():
                    place = jnp.maximum(request, 0)
                    if layers:
                        source, target = block_ref.at[:, place], out_ref.at[:, c]
                    else:
                        source, target = block_ref.at[place], out_ref.at[c]
                    held = held_ref.at[n - capacity]
                    fetch = pltpu.make_async_copy(source, held, in_sems.at[n])
                    store = pltpu.make_async_copy(held, target, out_sems.at[n])
                    if stage == 0:
                        fetch.start()
                    elif stage == 1:
                        fetch.wait()
                        store.start()
                    else:
                        store.wait()


def pack(picks, blocks, groups, layers):
    capacity = picks.shape[0] // groups
    rest = blocks.shape[2:] if layers else blocks.shape[1:]
    block = blocks.shape[:1] * layers + (capacity,) + rest
    held = (picks.shape[0] - capacity,) + blocks.shape[:1] * layers + rest
    return pl.pallas_call(
        functools.partial(pack_body, layers),
        grid=(1,),
        in_specs=[smem_spec(), any_spec()],
        out_specs=[hbm_spec()] * (groups - 1),
        out_shape=[pltpu.MemorySpace.HBM(block, BF16)] * (groups - 1),
        scratch_shapes=[
            pltpu.VMEM(held, BF16),
            pltpu.SemaphoreType.DMA((picks.shape[0],)),
            pltpu.SemaphoreType.DMA((picks.shape[0],)),
        ],
        compiler_params=params(),
        cost_estimate=cost(1024, 4 * blocks.size),
        name="pack",
    )(picks, in_hbm(blocks) if layers else blocks)


def choose_body(layer, source_ref, pick_ref, own_state_ref, own_factor_ref, *refs):
    slots = source_ref.shape[0]
    moved = (len(refs) - 5) // 2
    states, factors = refs[:moved], refs[moved : 2 * moved]
    out_ref, state_ref, factor_ref, state_sem, factor_sem = refs[2 * moved :]
    key_size, cols = state_ref.shape[1:]
    capacity = state_ref.shape[0] // (moved + 1)
    pieces = out_ref.shape[0]
    key_rows = key_size // pieces
    halves = cols // 128
    copies = []
    for c in range(capacity):
        request = jnp.maximum(pick_ref[c], 0)
        copies.append((own_state_ref.at[layer, request], state_ref.at[c], state_sem.at[c]))
        copies.append((own_factor_ref.at[request], factor_ref.at[c], factor_sem.at[c]))
    for g in range(moved):
        for c in range(capacity):
            n = (g + 1) * capacity + c
            copies.append((states[g].at[layer, c], state_ref.at[n], state_sem.at[n]))
            copies.append((factors[g].at[c], factor_ref.at[n], factor_sem.at[n]))
    copies = [pltpu.make_async_copy(*copy) for copy in copies]
    for copy in copies:
        copy.start()
    for copy in copies:
        copy.wait()
    steps = factor_ref.shape[1] // 3
    for t in range(slots):
        n = source_ref[t]
        block = factor_ref[n]
        update = lax.dot_general(
            block[:steps], block[steps : 2 * steps], (((0,), (0,)), ((), ())),
            preferred_element_type=F32,
        )
        kept = block[2 * steps :].astype(F32)
        kept = kept[0:1] + kept[1:2]
        chosen = (state_ref[n].astype(F32) * kept + update).astype(BF16)
        for j in range(pieces):
            for h in range(halves):
                low = (t * halves + h) * key_rows
                out_ref[j, low : low + key_rows] = chosen[
                    j * key_rows : (j + 1) * key_rows, h * 128 : (h + 1) * 128
                ]


def choose(layer, sources, picks, own_states, own_factors, states, factors, pieces):
    slots = sources.shape[0]
    key_size, cols = own_states.shape[2:]
    count = picks.shape[0]
    block = (pieces, slots * key_size * cols // (pieces * 128), 128)
    return pl.pallas_call(
        functools.partial(choose_body, layer),
        grid=(1,),
        in_specs=[smem_spec(), smem_spec()] + [hbm_spec()] * (2 + 2 * len(states)),
        out_specs=whole(block),
        out_shape=jax.ShapeDtypeStruct(block, BF16),
        scratch_shapes=[
            pltpu.VMEM((count, key_size, cols), BF16),
            pltpu.VMEM((count,) + own_factors.shape[1:], BF16),
            pltpu.SemaphoreType.DMA((count,)),
            pltpu.SemaphoreType.DMA((count,)),
        ],
        compiler_params=params(),
        cost_estimate=cost(1024 * 1024, 4 * 1024 * 1024),
        name="choose",
    )(sources, picks, *[in_hbm(block) for block in (own_states, own_factors, *states, *factors)])


def finish_body(piece_ref, hidden_ref, weight_ref, base_ref, *refs):
    states = refs[:-3]
    out_ref, cut_ref, sems = refs[-3:]
    pieces, rows = cut_ref.shape[0], cut_ref.shape[1]
    own_rows = base_ref.shape[0]
    copies = []
    for n, state_ref in enumerate(states):
        span = pl.ds(rows + n * state_ref.shape[1], state_ref.shape[1])
        copies.append(pltpu.make_async_copy(state_ref, out_ref.at[:, span], sems.at[n]))
        copies[-1].start()
    result = jnp.dot(hidden_ref[...], weight_ref[0], preferred_element_type=F32)
    base = jnp.concatenate([base_ref[...].astype(F32)] * (rows // own_rows), axis=0)
    row = lax.broadcasted_iota(jnp.int32, (rows, 1), 0)
    owned = row // own_rows == piece_ref[0]
    result = (result + jnp.where(owned, base, 0.0)).astype(BF16)
    for i in range(pieces):
        cut_ref[i] = result[:, i * 128 : (i + 1) * 128]
    copies.append(
        pltpu.make_async_copy(cut_ref, out_ref.at[:, pl.ds(0, rows)], sems.at[len(states)])
    )
    copies[-1].start()
    for copy in copies:
        copy.wait()


def finish(layer, piece, hidden, weights, base, states):
    rows, cols = hidden.shape
    width = weights.shape[2]
    pieces, state_rows = states[0].shape[0], states[0].shape[1]
    return pl.pallas_call(
        finish_body,
        grid=(1,),
        in_specs=[
            smem_spec(), whole(hidden.shape), layer_block(weights.shape[1:], layer),
            whole(base.shape),
        ]
        + [any_spec()] * len(states),
        out_specs=hbm_spec(),
        out_shape=jax.ShapeDtypeStruct((pieces, rows + state_rows * len(states), 128), BF16),
        scratch_shapes=[
            pltpu.VMEM((pieces, rows, 128), BF16),
            pltpu.SemaphoreType.DMA((len(states) + 1,)),
        ],
        compiler_params=params(),
        cost_estimate=cost(2 * rows * cols * width, 6 * 1024 * 1024),
        name="finish",
    )(piece, hidden, weights, base, *states)


def deliver_body(landed_ref, valid_ref, hidden_ref, home_ref):
    pieces = landed_ref.shape[0]
    rows = hidden_ref.shape[0]
    layers, slots, key_rows, columns = home_ref.shape
    halves = columns // (pieces * 128)
    total = jnp.zeros(hidden_ref.shape, F32)
    for i in range(pieces):
        total = total + landed_ref[i, :rows].astype(F32)
    hidden_ref[...] = jnp.where(valid_ref[...] > 0, total, 0.0).astype(BF16)
    for i in range(pieces):
        for layer in range(layers):
            for t in range(slots):
                for h in range(halves):
                    low = rows + ((layer * slots + t) * halves + h) * key_rows
                    start = (i * halves + h) * 128
                    home_ref[layer, t, :, start : start + 128] = landed_ref[
                        i, low : low + key_rows
                    ]


def deliver(landed, valid, home_shape):
    rows = valid.shape[0]
    return pl.pallas_call(
        deliver_body,
        grid=(1,),
        in_specs=[whole(landed.shape), whole(valid.shape)],
        out_specs=[whole((rows, 128)), whole(home_shape)],
        out_shape=[
            jax.ShapeDtypeStruct((rows, 128), BF16),
            jax.ShapeDtypeStruct(home_shape, BF16),
        ],
        compiler_params=params(),
        cost_estimate=cost(1024, 6 * 1024 * 1024),
        name="deliver",
    )(landed, valid)


def shards(
    hidden_in,
    draft_len,
    accepted,
    pos_offset,
    owner,
    init_state,
    norm_gain,
    w_query,
    w_key,
    w_value,
    w_gate,
    w_out,
    w_up,
    w_down,
):
    groups = lax.axis_size("req")
    pieces = lax.axis_size("mlp")
    my_group = lax.axis_index("req")
    my_piece = lax.axis_index("mlp")
    tok_rows = hidden_in.shape[0]
    width = hidden_in.shape[1] * pieces
    req_rows = draft_len.shape[0]
    slots = tok_rows // req_rows
    own_rows = tok_rows // pieces
    block_cols = w_value.shape[2]
    key_rows = K // pieces
    head_span = pieces // H
    head_index = my_piece // head_span
    upper_half = (my_piece % head_span).astype(jnp.int32).reshape(1)
    decays = 1.0 - jnp.exp2(-5.0 - jnp.arange(H, dtype=F32))
    log_decay = jnp.log(jnp.sum(jnp.where(jnp.arange(H) == head_index, decays, 0.0)))

    token = jnp.arange(tok_rows, dtype=jnp.int32)
    step = (token % slots).astype(F32)
    first = token // slots
    slot_steps = jnp.arange(slots, dtype=jnp.int32)
    positions = (pos_offset[:, None] + slot_steps[None, :]).reshape(tok_rows).astype(F32)
    valid_rows = (slot_steps[None, :] < draft_len[:, None]).reshape(tok_rows)
    halfway = K // 2
    frequencies = jnp.exp(jnp.arange(halfway, dtype=F32) * (-math.log(10000.0) / halfway))
    angles = positions[:, None] * frequencies[None, :]
    cosine, sine = jnp.cos(angles), jnp.sin(angles)
    grown = jnp.exp((step + 1.0) * log_decay)[:, None]
    shrink = jnp.exp(-(step + 1.0) * log_decay)[None, :]
    inside = (first[:, None] == first[None, :]) & (step[:, None] >= step[None, :])
    tables = jnp.stack(
        [
            cosine * grown,
            sine * grown,
            cosine * K ** (-0.5),
            sine * K ** (-0.5),
            jnp.where(inside, shrink, 0.0),
        ]
    )
    taken_count = accepted.astype(F32)
    taken_rows = jnp.repeat(taken_count, slots)
    gap = taken_rows - 1.0 - step
    weights = jnp.stack(
        [
            jnp.where(gap >= 0, jnp.exp(jnp.maximum(gap, 0.0) * log_decay), 0.0),
            jnp.exp(taken_rows * log_decay),
        ],
        axis=1,
    )

    capacity = 2 * req_rows // groups
    everyone = jnp.arange(owner.shape[0], dtype=jnp.int32)
    all_group = everyone // req_rows
    all_target = owner // req_rows
    peer_mask = (
        (all_group[:, None] == all_group[None, :])
        & (all_target[:, None] == all_target[None, :])
        & (everyone[None, :] < everyone[:, None])
    )
    all_place = jnp.sum(peer_mask.astype(jnp.int32), axis=1)
    step_groups = my_group ^ jnp.arange(groups, dtype=jnp.int32)
    place_ids = jnp.arange(capacity, dtype=jnp.int32)
    at_place = all_place[None, None, :] == place_ids[None, :, None]
    goes = (
        (all_group == my_group)[None, None, :]
        & (all_target[None, None, :] == step_groups[:, None, None])
        & at_place
    )
    picks = jnp.sum(jnp.where(goes, everyone % req_rows + 1, 0), axis=2).reshape(-1) - 1
    comes = (
        (all_target == my_group)[None, None, :]
        & (all_group[None, None, :] == step_groups[:, None, None])
        & at_place
    )
    fills = jnp.sum(jnp.where(comes, owner % req_rows + 1, 0), axis=2).reshape(-1) - 1

    slot_ids = jnp.arange(req_rows, dtype=jnp.int32)
    sources = jnp.sum(
        jnp.where(fills[None, :] == slot_ids[:, None], jnp.arange(fills.shape[0]), 0), axis=1
    ).astype(jnp.int32)

    copies = jnp.broadcast_to(hidden_in[None], (pieces,) + hidden_in.shape)
    full_rows = exchange(copies).transpose(1, 0, 2).reshape(tok_rows, width)
    states = send(pack(picks, init_state, groups, 1))
    stream = lax.dynamic_slice_in_dim(full_rows, my_piece * own_rows, own_rows)
    normed = layer_norm(full_rows, norm_gain[0, 0])
    home_shape = (LAYERS, req_rows, key_rows, pieces * block_cols)
    chosen = []
    for layer in range(LAYERS):
        last = layer + 1 == LAYERS
        query_part = jnp.dot(normed, w_query[layer], preferred_element_type=F32)
        key_part = jnp.dot(normed, w_key[layer], preferred_element_type=F32)
        own = jnp.stack([query_part, key_part]).astype(BF16)
        other = swap(own, "mlp", 1)
        values = jnp.dot(normed, w_value[layer], preferred_element_type=F32).astype(BF16)
        gate_values = jnp.dot(normed, w_gate[layer], preferred_element_type=F32)
        retained, moments, own_factors = retention(
            layer, upper_half, own, other, tables, weights, values, init_state
        )
        theirs = swap(moments, "mlp", 1)
        mixed = project(layer, pieces, retained, gate_values, moments, theirs, w_out)
        if not last:
            mixed, states = after(mixed, states, (4,))
        else:
            mixed, states = after(mixed, states, (7,))
            mixed, early = after(mixed, early, (7, 1))
        factors = send(pack(picks, own_factors, groups, 0))
        middle, spread_mid = settle(exchange(mixed), stream, norm_gain[layer, 1])
        if not last:
            spread_mid, states = after(spread_mid, states, (5,))
        else:
            spread_mid, states = after(spread_mid, states, (1,))
            spread_mid, factors = after(spread_mid, factors, (4, 5, 2, 3, 6, 7, 1))
        normed_mid = exchange(spread_mid).reshape(tok_rows, width)
        if last:
            for n, (own_part, parts) in enumerate(((early_own, early), (own_factors, factors))):
                chosen.append(
                    choose(
                        n, sources, picks, init_state, own_part, in_order(states),
                        in_order(parts), pieces,
                    )
                )
            tied = lax.optimization_barrier((normed_mid, *chosen))
            normed_mid, chosen = tied[0], tied[1:]
        hidden_units = jax.nn.gelu(
            jnp.dot(normed_mid, w_up[layer], preferred_element_type=F32), approximate=False
        ).astype(BF16)
        if not last:
            down_terms = jnp.dot(hidden_units, w_down[layer], preferred_element_type=F32)
            terms = down_terms.astype(BF16).reshape(pieces, own_rows, width)
            terms, states = after(terms, states, (2,))
            terms, factors = after(terms, factors, (4, 5))
            stream, spread_rows = settle(exchange(terms), middle, norm_gain[layer + 1, 0])
            spread_rows, states = after(spread_rows, states, (6,))
            spread_rows, factors = after(spread_rows, factors, (2, 3, 6))
            normed = exchange(spread_rows).reshape(tok_rows, width)
            normed, states = after(normed, states, (3,))
            early, early_own = factors, own_factors
    piece = my_piece.astype(jnp.int32).reshape(1)
    landed = exchange(finish(LAYERS - 1, piece, hidden_units, w_down, middle, chosen))
    valid = valid_rows.astype(jnp.int32)[:, None]
    return deliver(landed, valid, home_shape)


def solution(mesh):
    in_specs = (
        P("req", "mlp"),
        P("req"),
        P("req"),
        P("req"),
        P(),
        P(None, "req", None, "mlp"),
        P(),
        P(None, None, "mlp"),
        P(None, None, "mlp"),
        P(None, None, "mlp"),
        P(None, None, "mlp"),
        P(None, "mlp", None),
        P(None, None, "mlp"),
        P(None, "mlp", None),
    )
    out_specs = (P("req", "mlp"), P(None, "req", "mlp", None))
    return jax.shard_map(shards, mesh=mesh, in_specs=in_specs, out_specs=out_specs, check_vma=False)
```

```python
import functools
import math

import jax
import jax.numpy as jnp
from jax import lax
from jax.experimental import pallas as pl
from jax.experimental.pallas import tpu as pltpu
from jax.sharding import PartitionSpec as P

H = 8
K = 256
V = 512
LAYERS = 2

EPSILON = 1e-05
F32 = jnp.float32
BF16 = jnp.bfloat16
VMEM_BYTES = 48 * 1024 * 1024


def swap(value, axis, mask):
    pairs = [(source, source ^ mask) for source in range(lax.axis_size(axis))]
    return lax.ppermute(value, axis, pairs)


def send(blocks):
    return {mask: swap(block, "req", mask) for mask, block in enumerate(blocks, 1)}


def in_order(blocks):
    return [blocks[mask] for mask in sorted(blocks)]


def after(value, blocks, masks):
    tied = lax.optimization_barrier((value, *[blocks[n] for n in masks]))
    return tied[0], {**blocks, **dict(zip(masks, tied[1:]))}


def exchange(blocks):
    return lax.all_to_all(blocks, "mlp", split_axis=0, concat_axis=0, tiled=True)


def layer_norm(values, scales):
    widened = values.astype(F32)
    center = jnp.mean(widened, axis=-1, keepdims=True)
    shifted = widened - center
    variance = jnp.mean(shifted * shifted, axis=-1, keepdims=True)
    return (shifted * lax.rsqrt(variance + EPSILON) * scales).astype(BF16)


def any_spec():
    return pl.BlockSpec(memory_space=pl.ANY)


def in_hbm(block):
    return pltpu.with_memory_space_constraint(block, pltpu.MemorySpace.HBM)


def hbm_spec():
    return pl.BlockSpec(memory_space=pltpu.MemorySpace.HBM)


def smem_spec():
    return pl.BlockSpec(memory_space=pltpu.SMEM)


def whole(shape):
    return pl.BlockSpec(shape, lambda i: (0,) * len(shape))


def layer_block(shape, layer):
    return pl.BlockSpec((1,) + shape, lambda i: (layer,) + (0,) * len(shape))


def params():
    return pltpu.CompilerParams(vmem_limit_bytes=VMEM_BYTES)


def cost(flops, nbytes):
    return pl.CostEstimate(flops=flops, bytes_accessed=nbytes, transcendentals=0)


def query_key_body(layer, row_ref, query_ref, key_ref, out_ref, held_ref, sems):
    chunks, span = held_ref.shape[1], held_ref.shape[2]
    copies = []
    for n, ref in enumerate((query_ref, key_ref)):
        for c in range(chunks):
            copies.append(
                pltpu.make_async_copy(
                    ref.at[layer, pl.ds(c * span, span)], held_ref.at[n, c], sems.at[n, c]
                )
            )
            copies[-1].start()
    for n in range(2):
        total = None
        for c in range(chunks):
            copies[n * chunks + c].wait()
            part = jnp.dot(
                row_ref[:, c * span : (c + 1) * span], held_ref[n, c],
                preferred_element_type=F32,
            )
            total = part if total is None else total + part
        out_ref[n] = total.astype(BF16)


def query_key(layer, rows, w_query, w_key):
    cols, depth = w_query.shape[2], w_query.shape[1]
    chunks = 4
    block = (2, rows.shape[0], cols)
    return pl.pallas_call(
        functools.partial(query_key_body, layer),
        grid=(1,),
        in_specs=[whole(rows.shape), any_spec(), any_spec()],
        out_specs=whole(block),
        out_shape=jax.ShapeDtypeStruct(block, BF16),
        scratch_shapes=[
            pltpu.VMEM((2, chunks, depth // chunks, cols), BF16),
            pltpu.SemaphoreType.DMA((2, chunks)),
        ],
        compiler_params=params(),
        cost_estimate=cost(4 * rows.size * cols, 2 * 1024 * 1024),
        name="query_key",
    )(rows, in_hbm(w_query), in_hbm(w_key))


def hidden_units(layer, row_ref, up_ref, down_ref, up_held, down_held, up_sems, down_sem):
    chunks, span = up_held.shape[0], up_held.shape[1]
    copies = []
    for c in range(chunks):
        copies.append(
            pltpu.make_async_copy(
                up_ref.at[layer, pl.ds(c * span, span)], up_held.at[c], up_sems.at[c]
            )
        )
        copies[-1].start()
    down_copy = pltpu.make_async_copy(down_ref.at[layer], down_held, down_sem)
    down_copy.start()
    total = None
    for c in range(chunks):
        copies[c].wait()
        part = jnp.dot(
            row_ref[:, c * span : (c + 1) * span], up_held[c], preferred_element_type=F32
        )
        total = part if total is None else total + part
    active = 0.5 * total * (1.0 + lax.erf(total * math.sqrt(0.5)))
    down_copy.wait()
    return active.astype(BF16)


def mlp_scratch(w_up, w_down):
    chunks = 4
    return [
        pltpu.VMEM((chunks, w_up.shape[1] // chunks, w_up.shape[2]), BF16),
        pltpu.VMEM(w_down.shape[1:], BF16),
        pltpu.SemaphoreType.DMA((chunks,)),
        pltpu.SemaphoreType.DMA(()),
    ]


def feed_body(layer, row_ref, up_ref, down_ref, out_ref, *held):
    active = hidden_units(layer, row_ref, up_ref, down_ref, *held)
    result = jnp.dot(active, held[1][...], preferred_element_type=F32)
    own_rows = out_ref.shape[1]
    for i in range(out_ref.shape[0]):
        out_ref[i] = result[i * own_rows : (i + 1) * own_rows].astype(BF16)


def feed(layer, pieces, rows, w_up, w_down):
    count, width = rows.shape
    block = (pieces, count // pieces, width)
    return pl.pallas_call(
        functools.partial(feed_body, layer),
        grid=(1,),
        in_specs=[whole(rows.shape), any_spec(), any_spec()],
        out_specs=whole(block),
        out_shape=jax.ShapeDtypeStruct(block, BF16),
        scratch_shapes=mlp_scratch(w_up, w_down),
        compiler_params=params(),
        cost_estimate=cost(4 * rows.size * w_up.shape[2], 3 * 1024 * 1024),
        name="feed",
    )(rows, in_hbm(w_up), in_hbm(w_down))


def retention_body(
    half_ref, own_ref, other_ref, table_ref, weight_ref, value_ref, state_ref,
    retained_ref, moment_ref, factor_ref,
):
    upper = half_ref[0] == 1
    requests = state_ref.shape[1]
    rows = value_ref.shape[0]
    slots = rows // requests
    own_q, own_k = own_ref[0].astype(F32), own_ref[1].astype(F32)
    other_q, other_k = other_ref[0].astype(F32), other_ref[1].astype(F32)
    q_low, q_high = jnp.where(upper, other_q, own_q), jnp.where(upper, own_q, other_q)
    k_low, k_high = jnp.where(upper, other_k, own_k), jnp.where(upper, own_k, other_k)
    q_cos, q_sin, k_cos, k_sin = table_ref[0], table_ref[1], table_ref[2], table_ref[3]
    queries = jnp.concatenate(
        [q_low * q_cos - q_high * q_sin, q_high * q_cos + q_low * q_sin], axis=1
    ).astype(BF16)
    keys = jnp.concatenate(
        [k_low * k_cos - k_high * k_sin, k_high * k_cos + k_low * k_sin], axis=1
    )
    values = value_ref[...]
    scores = lax.dot_general(
        queries, keys.astype(BF16), (((1,), (1,)), ((), ())), preferred_element_type=F32
    )
    scores = (scores * table_ref[4]).astype(BF16)
    inner = jnp.dot(scores, values, preferred_element_type=F32)
    parts = []
    for r in range(requests):
        low, high = r * slots, (r + 1) * slots
        parts.append(
            inner[low:high]
            + jnp.dot(queries[low:high], state_ref[0, r], preferred_element_type=F32)
        )
    retained = jnp.concatenate(parts, axis=0)
    retained_ref[...] = retained
    lane = lax.broadcasted_iota(jnp.int32, (rows, 128), 1)
    total = jnp.sum(retained, axis=1, keepdims=True)
    squares = jnp.sum(retained * retained, axis=1, keepdims=True)
    columns = jnp.where(lane == 0, total, jnp.where(lane == 1, squares, 0.0))
    moment_ref[...] = jnp.transpose(columns)[:8]
    weighted = (keys * weight_ref[:, 0:1]).astype(BF16)
    kept = weight_ref[:, 1:2]
    rough = kept.astype(BF16)
    rest = (kept - rough.astype(F32)).astype(BF16)
    first = lax.broadcasted_iota(jnp.int32, (rows, 1), 0) % slots == 0
    kept = jnp.where(first, rough.astype(F32), rest.astype(F32))
    kept = jnp.broadcast_to(kept, keys.shape).astype(BF16)
    for r in range(requests):
        low, high = r * slots, (r + 1) * slots
        for n, part in enumerate((weighted, values, kept)):
            factor_ref[r, n * slots : (n + 1) * slots] = part[low:high]


def retention(layer, half, own, other, tables, weights, values, states):
    rows, cols = values.shape
    requests, key_size = states.shape[1], states.shape[2]
    factors = (requests, 3 * rows // requests, key_size)
    return pl.pallas_call(
        retention_body,
        grid=(1,),
        in_specs=[
            smem_spec(), whole(own.shape), whole(other.shape), whole(tables.shape),
            whole(weights.shape), whole(values.shape), layer_block(states.shape[1:], layer),
        ],
        out_specs=[whole((rows, cols)), whole((8, rows)), whole(factors)],
        out_shape=[
            jax.ShapeDtypeStruct((rows, cols), F32),
            jax.ShapeDtypeStruct((8, rows), F32),
            jax.ShapeDtypeStruct(factors, BF16),
        ],
        compiler_params=params(),
        cost_estimate=cost(4 * rows * key_size * cols, 2 * 1024 * 1024),
        name="retention",
    )(half, own, other, tables, weights, values, states)


def project_body(retained_ref, gate_ref, mine_ref, theirs_ref, weight_ref, out_ref):
    pieces, own_rows, width = out_ref.shape
    rows = retained_ref.shape[0]
    sums = mine_ref[...] + theirs_ref[...]
    padded = jnp.concatenate([sums, jnp.zeros((128 - 8, rows), F32)], axis=0)
    columns = jnp.transpose(padded)
    center = columns[:, 0:1] / V
    variance = columns[:, 1:2] / V - center * center
    gate = gate_ref[...]
    mixed = (retained_ref[...] - center) * lax.rsqrt(variance + EPSILON)
    mixed = (mixed * (gate / (1.0 + jnp.exp(-gate)))).astype(BF16)
    result = jnp.dot(mixed, weight_ref[0], preferred_element_type=F32)
    for i in range(pieces):
        out_ref[i] = result[i * own_rows : (i + 1) * own_rows].astype(BF16)


def project(layer, pieces, retained, gate, mine, theirs, weights):
    rows, cols = retained.shape
    width = weights.shape[2]
    block = (pieces, rows // pieces, width)
    return pl.pallas_call(
        project_body,
        grid=(1,),
        in_specs=[
            whole((rows, cols)), whole((rows, cols)), whole(mine.shape), whole(theirs.shape),
            layer_block(weights.shape[1:], layer),
        ],
        out_specs=whole(block),
        out_shape=jax.ShapeDtypeStruct(block, BF16),
        compiler_params=params(),
        cost_estimate=cost(2 * rows * cols * width, 2 * 1024 * 1024),
        name="project",
    )(retained, gate, mine, theirs, weights)


def settle_body(term_ref, base_ref, gain_ref, sum_ref, out_ref):
    pieces, own_rows, width = term_ref.shape
    total = jnp.zeros((own_rows, width), F32)
    for i in range(pieces):
        total = total + term_ref[i].astype(F32)
    rounded = (base_ref[...].astype(F32) + total).astype(BF16)
    sum_ref[...] = rounded
    widened = rounded.astype(F32)
    shifted = widened - jnp.mean(widened, axis=-1, keepdims=True)
    variance = jnp.mean(shifted * shifted, axis=-1, keepdims=True)
    normed = (shifted * lax.rsqrt(variance + EPSILON) * gain_ref[...]).astype(BF16)
    for i in range(pieces):
        out_ref[i] = normed


def settle(terms, base, gain):
    width = terms.shape[2]
    return pl.pallas_call(
        settle_body,
        grid=(1,),
        in_specs=[whole(terms.shape), whole(base.shape), whole((1, width))],
        out_specs=[whole(base.shape), whole(terms.shape)],
        out_shape=[
            jax.ShapeDtypeStruct(base.shape, BF16),
            jax.ShapeDtypeStruct(terms.shape, BF16),
        ],
        compiler_params=params(),
        cost_estimate=cost(4 * terms.size, 1024 * 1024),
        name="settle",
    )(terms, base, gain.reshape(1, width))


def pack_body(layers, pick_ref, block_ref, *refs):
    outs, held_ref, in_sems, out_sems = refs[:-3], refs[-3], refs[-2], refs[-1]
    capacity = outs[0].shape[1 if layers else 0]
    for stage in range(3):
        for g, out_ref in enumerate(outs):
            for c in range(capacity):
                n = (g + 1) * capacity + c
                request = pick_ref[n]

                @pl.when(request >= 0)
                def _():
                    place = jnp.maximum(request, 0)
                    if layers:
                        source, target = block_ref.at[:, place], out_ref.at[:, c]
                    else:
                        source, target = block_ref.at[place], out_ref.at[c]
                    held = held_ref.at[n - capacity]
                    fetch = pltpu.make_async_copy(source, held, in_sems.at[n])
                    store = pltpu.make_async_copy(held, target, out_sems.at[n])
                    if stage == 0:
                        fetch.start()
                    elif stage == 1:
                        fetch.wait()
                        store.start()
                    else:
                        store.wait()


def pack(picks, blocks, groups, layers):
    capacity = picks.shape[0] // groups
    rest = blocks.shape[2:] if layers else blocks.shape[1:]
    block = blocks.shape[:1] * layers + (capacity,) + rest
    held = (picks.shape[0] - capacity,) + blocks.shape[:1] * layers + rest
    return pl.pallas_call(
        functools.partial(pack_body, layers),
        grid=(1,),
        in_specs=[smem_spec(), any_spec()],
        out_specs=[hbm_spec()] * (groups - 1),
        out_shape=[pltpu.MemorySpace.HBM(block, BF16)] * (groups - 1),
        scratch_shapes=[
            pltpu.VMEM(held, BF16),
            pltpu.SemaphoreType.DMA((picks.shape[0],)),
            pltpu.SemaphoreType.DMA((picks.shape[0],)),
        ],
        compiler_params=params(),
        cost_estimate=cost(1024, 4 * blocks.size),
        name="pack",
    )(picks, in_hbm(blocks) if layers else blocks)


def choose_body(layer, source_ref, pick_ref, own_state_ref, own_factor_ref, *refs):
    slots = source_ref.shape[0]
    moved = (len(refs) - 5) // 2
    states, factors = refs[:moved], refs[moved : 2 * moved]
    out_ref, state_ref, factor_ref, state_sem, factor_sem = refs[2 * moved :]
    key_size, cols = state_ref.shape[1:]
    capacity = state_ref.shape[0] // (moved + 1)
    pieces = out_ref.shape[0]
    key_rows = key_size // pieces
    halves = cols // 128
    copies = []
    for c in range(capacity):
        request = jnp.maximum(pick_ref[c], 0)
        copies.append((own_state_ref.at[layer, request], state_ref.at[c], state_sem.at[c]))
        copies.append((own_factor_ref.at[request], factor_ref.at[c], factor_sem.at[c]))
    for g in range(moved):
        for c in range(capacity):
            n = (g + 1) * capacity + c
            copies.append((states[g].at[layer, c], state_ref.at[n], state_sem.at[n]))
            copies.append((factors[g].at[c], factor_ref.at[n], factor_sem.at[n]))
    copies = [pltpu.make_async_copy(*copy) for copy in copies]
    for copy in copies:
        copy.start()
    for copy in copies:
        copy.wait()
    steps = factor_ref.shape[1] // 3
    for t in range(slots):
        n = source_ref[t]
        block = factor_ref[n]
        update = lax.dot_general(
            block[:steps], block[steps : 2 * steps], (((0,), (0,)), ((), ())),
            preferred_element_type=F32,
        )
        kept = block[2 * steps :].astype(F32)
        kept = kept[0:1] + kept[1:2]
        chosen = (state_ref[n].astype(F32) * kept + update).astype(BF16)
        for j in range(pieces):
            for h in range(halves):
                low = (t * halves + h) * key_rows
                out_ref[j, low : low + key_rows] = chosen[
                    j * key_rows : (j + 1) * key_rows, h * 128 : (h + 1) * 128
                ]


def choose(layer, sources, picks, own_states, own_factors, states, factors, pieces):
    slots = sources.shape[0]
    key_size, cols = own_states.shape[2:]
    count = picks.shape[0]
    block = (pieces, slots * key_size * cols // (pieces * 128), 128)
    return pl.pallas_call(
        functools.partial(choose_body, layer),
        grid=(1,),
        in_specs=[smem_spec(), smem_spec()] + [hbm_spec()] * (2 + 2 * len(states)),
        out_specs=whole(block),
        out_shape=jax.ShapeDtypeStruct(block, BF16),
        scratch_shapes=[
            pltpu.VMEM((count, key_size, cols), BF16),
            pltpu.VMEM((count,) + own_factors.shape[1:], BF16),
            pltpu.SemaphoreType.DMA((count,)),
            pltpu.SemaphoreType.DMA((count,)),
        ],
        compiler_params=params(),
        cost_estimate=cost(1024 * 1024, 4 * 1024 * 1024),
        name="choose",
    )(sources, picks, *[in_hbm(block) for block in (own_states, own_factors, *states, *factors)])


def finish_body(layer, piece_ref, row_ref, base_ref, up_ref, down_ref, *refs):
    states, out_ref, cut_ref, sems = refs[:-7], refs[-7], refs[-6], refs[-5]
    held = refs[-4:]
    pieces, rows = cut_ref.shape[0], cut_ref.shape[1]
    own_rows = base_ref.shape[0]
    copies = []
    for n, state_ref in enumerate(states):
        span = pl.ds(rows + n * state_ref.shape[1], state_ref.shape[1])
        copies.append(pltpu.make_async_copy(state_ref, out_ref.at[:, span], sems.at[n]))
    active = hidden_units(layer, row_ref, up_ref, down_ref, *held)
    for copy in copies:
        copy.start()
    result = jnp.dot(active, held[1][...], preferred_element_type=F32)
    base = jnp.concatenate([base_ref[...].astype(F32)] * (rows // own_rows), axis=0)
    row = lax.broadcasted_iota(jnp.int32, (rows, 1), 0)
    owned = row // own_rows == piece_ref[0]
    result = (result + jnp.where(owned, base, 0.0)).astype(BF16)
    for i in range(pieces):
        cut_ref[i] = result[:, i * 128 : (i + 1) * 128]
    copies.append(
        pltpu.make_async_copy(cut_ref, out_ref.at[:, pl.ds(0, rows)], sems.at[len(states)])
    )
    copies[-1].start()
    for copy in copies:
        copy.wait()


def finish(layer, piece, rows, base, w_up, w_down, states):
    count = rows.shape[0]
    pieces, state_rows = states[0].shape[0], states[0].shape[1]
    return pl.pallas_call(
        functools.partial(finish_body, layer),
        grid=(1,),
        in_specs=[smem_spec(), whole(rows.shape), whole(base.shape), any_spec(), any_spec()]
        + [any_spec()] * len(states),
        out_specs=hbm_spec(),
        out_shape=jax.ShapeDtypeStruct((pieces, count + state_rows * len(states), 128), BF16),
        scratch_shapes=[
            pltpu.VMEM((pieces, count, 128), BF16),
            pltpu.SemaphoreType.DMA((len(states) + 1,)),
        ]
        + mlp_scratch(w_up, w_down),
        compiler_params=params(),
        cost_estimate=cost(4 * rows.size * w_up.shape[2], 7 * 1024 * 1024),
        name="finish",
    )(piece, rows, base, in_hbm(w_up), in_hbm(w_down), *states)


def deliver_body(landed_ref, valid_ref, hidden_ref, home_ref):
    pieces = landed_ref.shape[0]
    rows = hidden_ref.shape[0]
    layers, slots, key_rows, columns = home_ref.shape
    halves = columns // (pieces * 128)
    total = jnp.zeros(hidden_ref.shape, F32)
    for i in range(pieces):
        total = total + landed_ref[i, :rows].astype(F32)
    hidden_ref[...] = jnp.where(valid_ref[...] > 0, total, 0.0).astype(BF16)
    for i in range(pieces):
        for layer in range(layers):
            for t in range(slots):
                for h in range(halves):
                    low = rows + ((layer * slots + t) * halves + h) * key_rows
                    start = (i * halves + h) * 128
                    home_ref[layer, t, :, start : start + 128] = landed_ref[
                        i, low : low + key_rows
                    ]


def deliver(landed, valid, home_shape):
    rows = valid.shape[0]
    return pl.pallas_call(
        deliver_body,
        grid=(1,),
        in_specs=[whole(landed.shape), whole(valid.shape)],
        out_specs=[whole((rows, 128)), whole(home_shape)],
        out_shape=[
            jax.ShapeDtypeStruct((rows, 128), BF16),
            jax.ShapeDtypeStruct(home_shape, BF16),
        ],
        compiler_params=params(),
        cost_estimate=cost(1024, 6 * 1024 * 1024),
        name="deliver",
    )(landed, valid)


def shards(
    hidden_in,
    draft_len,
    accepted,
    pos_offset,
    owner,
    init_state,
    norm_gain,
    w_query,
    w_key,
    w_value,
    w_gate,
    w_out,
    w_up,
    w_down,
):
    groups = lax.axis_size("req")
    pieces = lax.axis_size("mlp")
    my_group = lax.axis_index("req")
    my_piece = lax.axis_index("mlp")
    tok_rows = hidden_in.shape[0]
    width = hidden_in.shape[1] * pieces
    req_rows = draft_len.shape[0]
    slots = tok_rows // req_rows
    own_rows = tok_rows // pieces
    block_cols = w_value.shape[2]
    key_rows = K // pieces
    head_span = pieces // H
    head_index = my_piece // head_span
    upper_half = (my_piece % head_span).astype(jnp.int32).reshape(1)
    decays = 1.0 - jnp.exp2(-5.0 - jnp.arange(H, dtype=F32))
    log_decay = jnp.log(jnp.sum(jnp.where(jnp.arange(H) == head_index, decays, 0.0)))

    token = jnp.arange(tok_rows, dtype=jnp.int32)
    step = (token % slots).astype(F32)
    first = token // slots
    slot_steps = jnp.arange(slots, dtype=jnp.int32)
    positions = (pos_offset[:, None] + slot_steps[None, :]).reshape(tok_rows).astype(F32)
    valid_rows = (slot_steps[None, :] < draft_len[:, None]).reshape(tok_rows)
    halfway = K // 2
    frequencies = jnp.exp(jnp.arange(halfway, dtype=F32) * (-math.log(10000.0) / halfway))
    angles = positions[:, None] * frequencies[None, :]
    cosine, sine = jnp.cos(angles), jnp.sin(angles)
    grown = jnp.exp((step + 1.0) * log_decay)[:, None]
    shrink = jnp.exp(-(step + 1.0) * log_decay)[None, :]
    inside = (first[:, None] == first[None, :]) & (step[:, None] >= step[None, :])
    tables = jnp.stack(
        [
            cosine * grown,
            sine * grown,
            cosine * K ** (-0.5),
            sine * K ** (-0.5),
            jnp.where(inside, shrink, 0.0),
        ]
    )
    taken_count = accepted.astype(F32)
    taken_rows = jnp.repeat(taken_count, slots)
    gap = taken_rows - 1.0 - step
    weights = jnp.stack(
        [
            jnp.where(gap >= 0, jnp.exp(jnp.maximum(gap, 0.0) * log_decay), 0.0),
            jnp.exp(taken_rows * log_decay),
        ],
        axis=1,
    )

    capacity = 2 * req_rows // groups
    everyone = jnp.arange(owner.shape[0], dtype=jnp.int32)
    all_group = everyone // req_rows
    all_target = owner // req_rows
    peer_mask = (
        (all_group[:, None] == all_group[None, :])
        & (all_target[:, None] == all_target[None, :])
        & (everyone[None, :] < everyone[:, None])
    )
    all_place = jnp.sum(peer_mask.astype(jnp.int32), axis=1)
    step_groups = my_group ^ jnp.arange(groups, dtype=jnp.int32)
    place_ids = jnp.arange(capacity, dtype=jnp.int32)
    at_place = all_place[None, None, :] == place_ids[None, :, None]
    goes = (
        (all_group == my_group)[None, None, :]
        & (all_target[None, None, :] == step_groups[:, None, None])
        & at_place
    )
    picks = jnp.sum(jnp.where(goes, everyone % req_rows + 1, 0), axis=2).reshape(-1) - 1
    comes = (
        (all_target == my_group)[None, None, :]
        & (all_group[None, None, :] == step_groups[:, None, None])
        & at_place
    )
    fills = jnp.sum(jnp.where(comes, owner % req_rows + 1, 0), axis=2).reshape(-1) - 1

    slot_ids = jnp.arange(req_rows, dtype=jnp.int32)
    sources = jnp.sum(
        jnp.where(fills[None, :] == slot_ids[:, None], jnp.arange(fills.shape[0]), 0), axis=1
    ).astype(jnp.int32)

    copies = jnp.broadcast_to(hidden_in[None], (pieces,) + hidden_in.shape)
    full_rows = exchange(copies).transpose(1, 0, 2).reshape(tok_rows, width)
    states = send(pack(picks, init_state, groups, 1))
    stream = lax.dynamic_slice_in_dim(full_rows, my_piece * own_rows, own_rows)
    normed = layer_norm(full_rows, norm_gain[0, 0])
    home_shape = (LAYERS, req_rows, key_rows, pieces * block_cols)
    chosen = []
    for layer in range(LAYERS):
        last = layer + 1 == LAYERS
        own = query_key(layer, normed, w_query, w_key)
        other = swap(own, "mlp", 1)
        values = jnp.dot(normed, w_value[layer], preferred_element_type=F32).astype(BF16)
        gate_values = jnp.dot(normed, w_gate[layer], preferred_element_type=F32)
        retained, moments, own_factors = retention(
            layer, upper_half, own, other, tables, weights, values, init_state
        )
        theirs = swap(moments, "mlp", 1)
        mixed = project(layer, pieces, retained, gate_values, moments, theirs, w_out)
        if not last:
            mixed, states = after(mixed, states, (2,))
        else:
            mixed, states = after(mixed, states, (7,))
            mixed, early = after(mixed, early, (7, 1))
        factors = send(pack(picks, own_factors, groups, 0))
        middle, spread_mid = settle(exchange(mixed), stream, norm_gain[layer, 1])
        if not last:
            spread_mid, states = after(spread_mid, states, (3,))
        else:
            spread_mid, states = after(spread_mid, states, (1,))
            spread_mid, factors = after(spread_mid, factors, (4, 5, 2, 3, 6, 7, 1))
        normed_mid = exchange(spread_mid).reshape(tok_rows, width)
        if last:
            for n, (own_part, parts) in enumerate(((early_own, early), (own_factors, factors))):
                chosen.append(
                    choose(
                        n, sources, picks, init_state, own_part, in_order(states),
                        in_order(parts), pieces,
                    )
                )
            tied = lax.optimization_barrier((normed_mid, *chosen))
            normed_mid, chosen = tied[0], tied[1:]
        if not last:
            terms = feed(layer, pieces, normed_mid, w_up, w_down)
            terms, states = after(terms, states, (4,))
            terms, factors = after(terms, factors, (4, 5))
            stream, spread_rows = settle(exchange(terms), middle, norm_gain[layer + 1, 0])
            spread_rows, states = after(spread_rows, states, (5,))
            spread_rows, factors = after(spread_rows, factors, (2, 3, 6))
            normed = exchange(spread_rows).reshape(tok_rows, width)
            normed, states = after(normed, states, (6,))
            early, early_own = factors, own_factors
    piece = my_piece.astype(jnp.int32).reshape(1)
    landed = exchange(finish(LAYERS - 1, piece, normed_mid, middle, w_up, w_down, chosen))
    valid = valid_rows.astype(jnp.int32)[:, None]
    return deliver(landed, valid, home_shape)


def solution(mesh):
    in_specs = (
        P("req", "mlp"),
        P("req"),
        P("req"),
        P("req"),
        P(),
        P(None, "req", None, "mlp"),
        P(),
        P(None, None, "mlp"),
        P(None, None, "mlp"),
        P(None, None, "mlp"),
        P(None, None, "mlp"),
        P(None, "mlp", None),
        P(None, None, "mlp"),
        P(None, "mlp", None),
    )
    out_specs = (P("req", "mlp"), P(None, "req", "mlp", None))
    return jax.shard_map(shards, mesh=mesh, in_specs=in_specs, out_specs=out_specs, check_vma=False)
```

```python
import functools
import math

import jax
import jax.numpy as jnp
from jax import lax
from jax.experimental import pallas as pl
from jax.experimental.pallas import tpu as pltpu
from jax.sharding import PartitionSpec as P

H = 8
K = 256
V = 512
LAYERS = 2

EPSILON = 1e-05
F32 = jnp.float32
BF16 = jnp.bfloat16
VMEM_BYTES = 48 * 1024 * 1024


def swap(value, axis, mask):
    pairs = [(source, source ^ mask) for source in range(lax.axis_size(axis))]
    return lax.ppermute(value, axis, pairs)


def send(blocks):
    return {mask: swap(block, "req", mask) for mask, block in enumerate(blocks, 1)}


def in_order(blocks):
    return [blocks[mask] for mask in sorted(blocks)]


def after(value, blocks, masks):
    tied = lax.optimization_barrier((value, *[blocks[n] for n in masks]))
    return tied[0], {**blocks, **dict(zip(masks, tied[1:]))}


def exchange(blocks):
    return lax.all_to_all(blocks, "mlp", split_axis=0, concat_axis=0, tiled=True)


def layer_norm(values, scales):
    widened = values.astype(F32)
    center = jnp.mean(widened, axis=-1, keepdims=True)
    shifted = widened - center
    variance = jnp.mean(shifted * shifted, axis=-1, keepdims=True)
    return (shifted * lax.rsqrt(variance + EPSILON) * scales).astype(BF16)


def any_spec():
    return pl.BlockSpec(memory_space=pl.ANY)


def in_hbm(block):
    return pltpu.with_memory_space_constraint(block, pltpu.MemorySpace.HBM)


def hbm_spec():
    return pl.BlockSpec(memory_space=pltpu.MemorySpace.HBM)


def smem_spec():
    return pl.BlockSpec(memory_space=pltpu.SMEM)


def whole(shape):
    return pl.BlockSpec(shape, lambda i: (0,) * len(shape))


def layer_block(shape, layer):
    return pl.BlockSpec((1,) + shape, lambda i: (layer,) + (0,) * len(shape))


def params():
    return pltpu.CompilerParams(vmem_limit_bytes=VMEM_BYTES)


def cost(flops, nbytes):
    return pl.CostEstimate(flops=flops, bytes_accessed=nbytes, transcendentals=0)


def query_key_body(layer, row_ref, query_ref, key_ref, out_ref, row_held, held_ref, row_sem, sems):
    chunks, span = held_ref.shape[0], held_ref.shape[1]
    cols = query_ref.shape[2]
    row_copy = pltpu.make_async_copy(row_ref, row_held, row_sem)
    row_copy.start()
    copies = []
    for c in range(chunks):
        for n, ref in enumerate((query_ref, key_ref)):
            copies.append(
                pltpu.make_async_copy(
                    ref.at[layer, pl.ds(c * span, span)],
                    held_ref.at[c, :, pl.ds(n * cols, cols)],
                    sems.at[n, c],
                )
            )
            copies[-1].start()
    row_copy.wait()
    total = None
    for c in range(chunks):
        copies[2 * c].wait()
        copies[2 * c + 1].wait()
        part = jnp.dot(
            row_held[:, c * span : (c + 1) * span], held_ref[c], preferred_element_type=F32
        )
        total = part if total is None else total + part
    out_ref[0] = total[:, :cols].astype(BF16)
    out_ref[1] = total[:, cols:].astype(BF16)


def query_key(layer, rows, w_query, w_key):
    cols, depth = w_query.shape[2], w_query.shape[1]
    chunks = 4
    block = (2, rows.shape[0], cols)
    return pl.pallas_call(
        functools.partial(query_key_body, layer),
        grid=(1,),
        in_specs=[any_spec()] * 3,
        out_specs=whole(block),
        out_shape=jax.ShapeDtypeStruct(block, BF16),
        scratch_shapes=[
            pltpu.VMEM(rows.shape, BF16),
            pltpu.VMEM((chunks, depth // chunks, 2 * cols), BF16),
            pltpu.SemaphoreType.DMA(()),
            pltpu.SemaphoreType.DMA((2, chunks)),
        ],
        compiler_params=params(),
        cost_estimate=cost(4 * rows.size * cols, 2 * 1024 * 1024),
        name="query_key",
    )(rows, in_hbm(w_query), in_hbm(w_key))


def repeat_body(block_ref, out_ref):
    for i in range(out_ref.shape[0]):
        out_ref[i] = block_ref[...]


def repeat(block, pieces):
    shape = (pieces,) + block.shape
    return pl.pallas_call(
        repeat_body,
        grid=(1,),
        in_specs=[whole(block.shape)],
        out_specs=whole(shape),
        out_shape=jax.ShapeDtypeStruct(shape, BF16),
        compiler_params=params(),
        cost_estimate=cost(1024, 1024 * 1024),
        name="repeat",
    )(block)


def hidden_units(layer, row_ref, up_ref, down_ref, up_held, down_held, row_held, up_sems, sems):
    chunks, span = up_held.shape[0], up_held.shape[1]
    copies = []
    for c in range(chunks):
        copies.append(
            pltpu.make_async_copy(
                up_ref.at[layer, pl.ds(c * span, span)], up_held.at[c], up_sems.at[c]
            )
        )
        copies[-1].start()
    row_copy = pltpu.make_async_copy(row_ref, row_held, sems.at[0])
    row_copy.start()
    down_copy = pltpu.make_async_copy(down_ref.at[layer], down_held, sems.at[1])
    down_copy.start()
    row_copy.wait()
    total = None
    for c in range(chunks):
        copies[c].wait()
        part = jnp.dot(
            row_held[:, c * span : (c + 1) * span], up_held[c], preferred_element_type=F32
        )
        total = part if total is None else total + part
    active = 0.5 * total * (1.0 + lax.erf(total * math.sqrt(0.5)))
    down_copy.wait()
    return active.astype(BF16)


def mlp_scratch(rows, w_up, w_down):
    chunks = 4
    return [
        pltpu.VMEM((chunks, w_up.shape[1] // chunks, w_up.shape[2]), BF16),
        pltpu.VMEM(w_down.shape[1:], BF16),
        pltpu.VMEM(rows.shape, BF16),
        pltpu.SemaphoreType.DMA((chunks,)),
        pltpu.SemaphoreType.DMA((2,)),
    ]


def feed_body(layer, row_ref, up_ref, down_ref, out_ref, *held):
    active = hidden_units(layer, row_ref, up_ref, down_ref, *held)
    result = jnp.dot(active, held[1][...], preferred_element_type=F32)
    own_rows = out_ref.shape[1]
    for i in range(out_ref.shape[0]):
        out_ref[i] = result[i * own_rows : (i + 1) * own_rows].astype(BF16)


def feed(layer, pieces, rows, w_up, w_down):
    count, width = rows.shape
    block = (pieces, count // pieces, width)
    return pl.pallas_call(
        functools.partial(feed_body, layer),
        grid=(1,),
        in_specs=[any_spec()] * 3,
        out_specs=whole(block),
        out_shape=jax.ShapeDtypeStruct(block, BF16),
        scratch_shapes=mlp_scratch(rows, w_up, w_down),
        compiler_params=params(),
        cost_estimate=cost(4 * rows.size * w_up.shape[2], 3 * 1024 * 1024),
        name="feed",
    )(rows, in_hbm(w_up), in_hbm(w_down))


def retention_body(
    half_ref, own_ref, other_ref, table_ref, weight_ref, value_ref, state_ref,
    retained_ref, moment_ref, factor_ref,
):
    upper = half_ref[0] == 1
    requests = state_ref.shape[1]
    rows = value_ref.shape[0]
    slots = rows // requests
    own_q, own_k = own_ref[0].astype(F32), own_ref[1].astype(F32)
    other_q, other_k = other_ref[0].astype(F32), other_ref[1].astype(F32)
    q_low, q_high = jnp.where(upper, other_q, own_q), jnp.where(upper, own_q, other_q)
    k_low, k_high = jnp.where(upper, other_k, own_k), jnp.where(upper, own_k, other_k)
    q_cos, q_sin, k_cos, k_sin = table_ref[0], table_ref[1], table_ref[2], table_ref[3]
    queries = jnp.concatenate(
        [q_low * q_cos - q_high * q_sin, q_high * q_cos + q_low * q_sin], axis=1
    ).astype(BF16)
    keys = jnp.concatenate(
        [k_low * k_cos - k_high * k_sin, k_high * k_cos + k_low * k_sin], axis=1
    )
    values = value_ref[...]
    scores = lax.dot_general(
        queries, keys.astype(BF16), (((1,), (1,)), ((), ())), preferred_element_type=F32
    )
    scores = (scores * table_ref[4]).astype(BF16)
    inner = jnp.dot(scores, values, preferred_element_type=F32)
    parts = []
    for r in range(requests):
        low, high = r * slots, (r + 1) * slots
        parts.append(
            inner[low:high]
            + jnp.dot(queries[low:high], state_ref[0, r], preferred_element_type=F32)
        )
    retained = jnp.concatenate(parts, axis=0)
    retained_ref[...] = retained
    lane = lax.broadcasted_iota(jnp.int32, (rows, 128), 1)
    total = jnp.sum(retained, axis=1, keepdims=True)
    squares = jnp.sum(retained * retained, axis=1, keepdims=True)
    columns = jnp.where(lane == 0, total, jnp.where(lane == 1, squares, 0.0))
    moment_ref[...] = jnp.transpose(columns)[:8]
    weighted = (keys * weight_ref[:, 0:1]).astype(BF16)
    kept = weight_ref[:, 1:2]
    rough = kept.astype(BF16)
    rest = (kept - rough.astype(F32)).astype(BF16)
    first = lax.broadcasted_iota(jnp.int32, (rows, 1), 0) % slots == 0
    kept = jnp.where(first, rough.astype(F32), rest.astype(F32))
    kept = jnp.broadcast_to(kept, keys.shape).astype(BF16)
    for r in range(requests):
        low, high = r * slots, (r + 1) * slots
        for n, part in enumerate((weighted, values, kept)):
            factor_ref[r, n * slots : (n + 1) * slots] = part[low:high]


def retention(layer, half, own, other, tables, weights, values, states):
    rows, cols = values.shape
    requests, key_size = states.shape[1], states.shape[2]
    factors = (requests, 3 * rows // requests, key_size)
    return pl.pallas_call(
        retention_body,
        grid=(1,),
        in_specs=[
            smem_spec(), whole(own.shape), whole(other.shape), whole(tables.shape),
            whole(weights.shape), whole(values.shape), layer_block(states.shape[1:], layer),
        ],
        out_specs=[whole((rows, cols)), whole((8, rows)), whole(factors)],
        out_shape=[
            jax.ShapeDtypeStruct((rows, cols), F32),
            jax.ShapeDtypeStruct((8, rows), F32),
            jax.ShapeDtypeStruct(factors, BF16),
        ],
        compiler_params=params(),
        cost_estimate=cost(4 * rows * key_size * cols, 2 * 1024 * 1024),
        name="retention",
    )(half, own, other, tables, weights, values, states)


def project_body(retained_ref, gate_ref, mine_ref, theirs_ref, weight_ref, out_ref):
    pieces, own_rows, width = out_ref.shape
    rows = retained_ref.shape[0]
    sums = mine_ref[...] + theirs_ref[...]
    padded = jnp.concatenate([sums, jnp.zeros((128 - 8, rows), F32)], axis=0)
    columns = jnp.transpose(padded)
    center = columns[:, 0:1] / V
    variance = columns[:, 1:2] / V - center * center
    gate = gate_ref[...]
    mixed = (retained_ref[...] - center) * lax.rsqrt(variance + EPSILON)
    mixed = (mixed * (gate / (1.0 + jnp.exp(-gate)))).astype(BF16)
    result = jnp.dot(mixed, weight_ref[0], preferred_element_type=F32)
    for i in range(pieces):
        out_ref[i] = result[i * own_rows : (i + 1) * own_rows].astype(BF16)


def project(layer, pieces, retained, gate, mine, theirs, weights):
    rows, cols = retained.shape
    width = weights.shape[2]
    block = (pieces, rows // pieces, width)
    return pl.pallas_call(
        project_body,
        grid=(1,),
        in_specs=[
            whole((rows, cols)), whole((rows, cols)), whole(mine.shape), whole(theirs.shape),
            layer_block(weights.shape[1:], layer),
        ],
        out_specs=whole(block),
        out_shape=jax.ShapeDtypeStruct(block, BF16),
        compiler_params=params(),
        cost_estimate=cost(2 * rows * cols * width, 2 * 1024 * 1024),
        name="project",
    )(retained, gate, mine, theirs, weights)


def settle_body(term_ref, base_ref, gain_ref, sum_ref, out_ref):
    pieces, own_rows, width = term_ref.shape
    total = jnp.zeros((own_rows, width), F32)
    for i in range(pieces):
        total = total + term_ref[i].astype(F32)
    rounded = (base_ref[...].astype(F32) + total).astype(BF16)
    sum_ref[...] = rounded
    widened = rounded.astype(F32)
    shifted = widened - jnp.mean(widened, axis=-1, keepdims=True)
    variance = jnp.mean(shifted * shifted, axis=-1, keepdims=True)
    normed = (shifted * lax.rsqrt(variance + EPSILON) * gain_ref[...]).astype(BF16)
    for i in range(pieces):
        out_ref[i] = normed


def settle(terms, base, gain):
    width = terms.shape[2]
    return pl.pallas_call(
        settle_body,
        grid=(1,),
        in_specs=[whole(terms.shape), whole(base.shape), whole((1, width))],
        out_specs=[whole(base.shape), whole(terms.shape)],
        out_shape=[
            jax.ShapeDtypeStruct(base.shape, BF16),
            jax.ShapeDtypeStruct(terms.shape, BF16),
        ],
        compiler_params=params(),
        cost_estimate=cost(4 * terms.size, 1024 * 1024),
        name="settle",
    )(terms, base, gain.reshape(1, width))


def pack_body(layers, pick_ref, block_ref, *refs):
    outs, held_ref, in_sems, out_sems = refs[:-3], refs[-3], refs[-2], refs[-1]
    capacity = outs[0].shape[1 if layers else 0]
    for stage in range(3):
        for g, out_ref in enumerate(outs):
            for c in range(capacity):
                n = (g + 1) * capacity + c
                request = pick_ref[n]

                @pl.when(request >= 0)
                def _():
                    place = jnp.maximum(request, 0)
                    if layers:
                        source, target = block_ref.at[:, place], out_ref.at[:, c]
                    else:
                        source, target = block_ref.at[place], out_ref.at[c]
                    held = held_ref.at[n - capacity]
                    fetch = pltpu.make_async_copy(source, held, in_sems.at[n])
                    store = pltpu.make_async_copy(held, target, out_sems.at[n])
                    if stage == 0:
                        fetch.start()
                    elif stage == 1:
                        fetch.wait()
                        store.start()
                    else:
                        store.wait()


def pack(picks, blocks, groups, layers):
    capacity = picks.shape[0] // groups
    rest = blocks.shape[2:] if layers else blocks.shape[1:]
    block = blocks.shape[:1] * layers + (capacity,) + rest
    held = (picks.shape[0] - capacity,) + blocks.shape[:1] * layers + rest
    return pl.pallas_call(
        functools.partial(pack_body, layers),
        grid=(1,),
        in_specs=[smem_spec(), any_spec()],
        out_specs=[hbm_spec()] * (groups - 1),
        out_shape=[pltpu.MemorySpace.HBM(block, BF16)] * (groups - 1),
        scratch_shapes=[
            pltpu.VMEM(held, BF16),
            pltpu.SemaphoreType.DMA((picks.shape[0],)),
            pltpu.SemaphoreType.DMA((picks.shape[0],)),
        ],
        compiler_params=params(),
        cost_estimate=cost(1024, 4 * blocks.size),
        name="pack",
    )(picks, in_hbm(blocks) if layers else blocks)


def choose_body(layer, source_ref, pick_ref, own_state_ref, own_factor_ref, *refs):
    slots = source_ref.shape[0]
    moved = (len(refs) - 5) // 2
    states, factors = refs[:moved], refs[moved : 2 * moved]
    out_ref, state_ref, factor_ref, state_sem, factor_sem = refs[2 * moved :]
    key_size, cols = state_ref.shape[1:]
    capacity = state_ref.shape[0] // (moved + 1)
    pieces = out_ref.shape[0]
    key_rows = key_size // pieces
    halves = cols // 128
    copies = []
    for c in range(capacity):
        request = jnp.maximum(pick_ref[c], 0)
        copies.append((own_state_ref.at[layer, request], state_ref.at[c], state_sem.at[c]))
        copies.append((own_factor_ref.at[request], factor_ref.at[c], factor_sem.at[c]))
    for g in range(moved):
        for c in range(capacity):
            n = (g + 1) * capacity + c
            copies.append((states[g].at[layer, c], state_ref.at[n], state_sem.at[n]))
            copies.append((factors[g].at[c], factor_ref.at[n], factor_sem.at[n]))
    copies = [pltpu.make_async_copy(*copy) for copy in copies]
    for copy in copies:
        copy.start()
    for copy in copies:
        copy.wait()
    steps = factor_ref.shape[1] // 3
    for t in range(slots):
        n = source_ref[t]
        block = factor_ref[n]
        update = lax.dot_general(
            block[:steps], block[steps : 2 * steps], (((0,), (0,)), ((), ())),
            preferred_element_type=F32,
        )
        kept = block[2 * steps :].astype(F32)
        kept = kept[0:1] + kept[1:2]
        chosen = (state_ref[n].astype(F32) * kept + update).astype(BF16)
        for j in range(pieces):
            for h in range(halves):
                low = (t * halves + h) * key_rows
                out_ref[j, low : low + key_rows] = chosen[
                    j * key_rows : (j + 1) * key_rows, h * 128 : (h + 1) * 128
                ]


def choose(layer, sources, picks, own_states, own_factors, states, factors, pieces):
    slots = sources.shape[0]
    key_size, cols = own_states.shape[2:]
    count = picks.shape[0]
    block = (pieces, slots * key_size * cols // (pieces * 128), 128)
    return pl.pallas_call(
        functools.partial(choose_body, layer),
        grid=(1,),
        in_specs=[smem_spec(), smem_spec()] + [hbm_spec()] * (2 + 2 * len(states)),
        out_specs=whole(block),
        out_shape=jax.ShapeDtypeStruct(block, BF16),
        scratch_shapes=[
            pltpu.VMEM((count, key_size, cols), BF16),
            pltpu.VMEM((count,) + own_factors.shape[1:], BF16),
            pltpu.SemaphoreType.DMA((count,)),
            pltpu.SemaphoreType.DMA((count,)),
        ],
        compiler_params=params(),
        cost_estimate=cost(1024 * 1024, 4 * 1024 * 1024),
        name="choose",
    )(sources, picks, *[in_hbm(block) for block in (own_states, own_factors, *states, *factors)])


def finish_body(layer, piece_ref, row_ref, base_ref, up_ref, down_ref, *refs):
    states, out_ref, cut_ref, sems = refs[:-8], refs[-8], refs[-7], refs[-6]
    held = refs[-5:]
    pieces, rows = cut_ref.shape[0], cut_ref.shape[1]
    own_rows = base_ref.shape[0]
    copies = []
    for n, state_ref in enumerate(states):
        span = pl.ds(rows + n * state_ref.shape[1], state_ref.shape[1])
        copies.append(pltpu.make_async_copy(state_ref, out_ref.at[:, span], sems.at[n]))
    active = hidden_units(layer, row_ref, up_ref, down_ref, *held)
    for copy in copies:
        copy.start()
    result = jnp.dot(active, held[1][...], preferred_element_type=F32)
    base = jnp.concatenate([base_ref[...].astype(F32)] * (rows // own_rows), axis=0)
    row = lax.broadcasted_iota(jnp.int32, (rows, 1), 0)
    owned = row // own_rows == piece_ref[0]
    result = (result + jnp.where(owned, base, 0.0)).astype(BF16)
    for i in range(pieces):
        cut_ref[i] = result[:, i * 128 : (i + 1) * 128]
    copies.append(
        pltpu.make_async_copy(cut_ref, out_ref.at[:, pl.ds(0, rows)], sems.at[len(states)])
    )
    copies[-1].start()
    for copy in copies:
        copy.wait()


def finish(layer, piece, rows, base, w_up, w_down, states):
    count = rows.shape[0]
    pieces, state_rows = states[0].shape[0], states[0].shape[1]
    return pl.pallas_call(
        functools.partial(finish_body, layer),
        grid=(1,),
        in_specs=[smem_spec(), any_spec(), whole(base.shape), any_spec(), any_spec()]
        + [any_spec()] * len(states),
        out_specs=hbm_spec(),
        out_shape=jax.ShapeDtypeStruct((pieces, count + state_rows * len(states), 128), BF16),
        scratch_shapes=[
            pltpu.VMEM((pieces, count, 128), BF16),
            pltpu.SemaphoreType.DMA((len(states) + 1,)),
        ]
        + mlp_scratch(rows, w_up, w_down),
        compiler_params=params(),
        cost_estimate=cost(4 * rows.size * w_up.shape[2], 7 * 1024 * 1024),
        name="finish",
    )(piece, rows, base, in_hbm(w_up), in_hbm(w_down), *states)


def deliver_body(landed_ref, valid_ref, hidden_ref, home_ref):
    pieces = landed_ref.shape[0]
    rows = hidden_ref.shape[0]
    layers, slots, key_rows, columns = home_ref.shape
    halves = columns // (pieces * 128)
    total = jnp.zeros(hidden_ref.shape, F32)
    for i in range(pieces):
        total = total + landed_ref[i, :rows].astype(F32)
    hidden_ref[...] = jnp.where(valid_ref[...] > 0, total, 0.0).astype(BF16)
    for i in range(pieces):
        for layer in range(layers):
            for t in range(slots):
                for h in range(halves):
                    low = rows + ((layer * slots + t) * halves + h) * key_rows
                    start = (i * halves + h) * 128
                    home_ref[layer, t, :, start : start + 128] = landed_ref[
                        i, low : low + key_rows
                    ]


def deliver(landed, valid, home_shape):
    rows = valid.shape[0]
    return pl.pallas_call(
        deliver_body,
        grid=(1,),
        in_specs=[whole(landed.shape), whole(valid.shape)],
        out_specs=[whole((rows, 128)), whole(home_shape)],
        out_shape=[
            jax.ShapeDtypeStruct((rows, 128), BF16),
            jax.ShapeDtypeStruct(home_shape, BF16),
        ],
        compiler_params=params(),
        cost_estimate=cost(1024, 6 * 1024 * 1024),
        name="deliver",
    )(landed, valid)


def shards(
    hidden_in,
    draft_len,
    accepted,
    pos_offset,
    owner,
    init_state,
    norm_gain,
    w_query,
    w_key,
    w_value,
    w_gate,
    w_out,
    w_up,
    w_down,
):
    groups = lax.axis_size("req")
    pieces = lax.axis_size("mlp")
    my_group = lax.axis_index("req")
    my_piece = lax.axis_index("mlp")
    tok_rows = hidden_in.shape[0]
    width = hidden_in.shape[1] * pieces
    req_rows = draft_len.shape[0]
    slots = tok_rows // req_rows
    own_rows = tok_rows // pieces
    block_cols = w_value.shape[2]
    key_rows = K // pieces
    head_span = pieces // H
    head_index = my_piece // head_span
    upper_half = (my_piece % head_span).astype(jnp.int32).reshape(1)
    decays = 1.0 - jnp.exp2(-5.0 - jnp.arange(H, dtype=F32))
    log_decay = jnp.log(jnp.sum(jnp.where(jnp.arange(H) == head_index, decays, 0.0)))

    token = jnp.arange(tok_rows, dtype=jnp.int32)
    step = (token % slots).astype(F32)
    first = token // slots
    slot_steps = jnp.arange(slots, dtype=jnp.int32)
    positions = (pos_offset[:, None] + slot_steps[None, :]).reshape(tok_rows).astype(F32)
    valid_rows = (slot_steps[None, :] < draft_len[:, None]).reshape(tok_rows)
    halfway = K // 2
    frequencies = jnp.exp(jnp.arange(halfway, dtype=F32) * (-math.log(10000.0) / halfway))
    angles = positions[:, None] * frequencies[None, :]
    cosine, sine = jnp.cos(angles), jnp.sin(angles)
    grown = jnp.exp((step + 1.0) * log_decay)[:, None]
    shrink = jnp.exp(-(step + 1.0) * log_decay)[None, :]
    inside = (first[:, None] == first[None, :]) & (step[:, None] >= step[None, :])
    tables = jnp.stack(
        [
            cosine * grown,
            sine * grown,
            cosine * K ** (-0.5),
            sine * K ** (-0.5),
            jnp.where(inside, shrink, 0.0),
        ]
    )
    taken_count = accepted.astype(F32)
    taken_rows = jnp.repeat(taken_count, slots)
    gap = taken_rows - 1.0 - step
    weights = jnp.stack(
        [
            jnp.where(gap >= 0, jnp.exp(jnp.maximum(gap, 0.0) * log_decay), 0.0),
            jnp.exp(taken_rows * log_decay),
        ],
        axis=1,
    )

    capacity = 2 * req_rows // groups
    everyone = jnp.arange(owner.shape[0], dtype=jnp.int32)
    all_group = everyone // req_rows
    all_target = owner // req_rows
    peer_mask = (
        (all_group[:, None] == all_group[None, :])
        & (all_target[:, None] == all_target[None, :])
        & (everyone[None, :] < everyone[:, None])
    )
    all_place = jnp.sum(peer_mask.astype(jnp.int32), axis=1)
    step_groups = my_group ^ jnp.arange(groups, dtype=jnp.int32)
    place_ids = jnp.arange(capacity, dtype=jnp.int32)
    at_place = all_place[None, None, :] == place_ids[None, :, None]
    goes = (
        (all_group == my_group)[None, None, :]
        & (all_target[None, None, :] == step_groups[:, None, None])
        & at_place
    )
    picks = jnp.sum(jnp.where(goes, everyone % req_rows + 1, 0), axis=2).reshape(-1) - 1
    comes = (
        (all_target == my_group)[None, None, :]
        & (all_group[None, None, :] == step_groups[:, None, None])
        & at_place
    )
    fills = jnp.sum(jnp.where(comes, owner % req_rows + 1, 0), axis=2).reshape(-1) - 1

    slot_ids = jnp.arange(req_rows, dtype=jnp.int32)
    sources = jnp.sum(
        jnp.where(fills[None, :] == slot_ids[:, None], jnp.arange(fills.shape[0]), 0), axis=1
    ).astype(jnp.int32)

    full_rows = exchange(repeat(hidden_in, pieces)).transpose(1, 0, 2).reshape(tok_rows, width)
    states = send(pack(picks, init_state, groups, 1))
    stream = lax.dynamic_slice_in_dim(full_rows, my_piece * own_rows, own_rows)
    normed = layer_norm(full_rows, norm_gain[0, 0])
    home_shape = (LAYERS, req_rows, key_rows, pieces * block_cols)
    for layer in range(LAYERS):
        last = layer + 1 == LAYERS
        own = query_key(layer, normed, w_query, w_key)
        other = swap(own, "mlp", 1)
        values = jnp.dot(normed, w_value[layer], preferred_element_type=F32).astype(BF16)
        gate_values = jnp.dot(normed, w_gate[layer], preferred_element_type=F32)
        retained, moments, own_factors = retention(
            layer, upper_half, own, other, tables, weights, values, init_state
        )
        theirs = swap(moments, "mlp", 1)
        mixed = project(layer, pieces, retained, gate_values, moments, theirs, w_out)
        if not last:
            pass
        else:
            mixed, states = after(mixed, states, (7,))
            mixed, early = after(mixed, early, (7, 1))
        factors = send(pack(picks, own_factors, groups, 0))
        middle, spread_mid = settle(exchange(mixed), stream, norm_gain[layer, 1])
        if not last:
            spread_mid, states = after(spread_mid, states, (2, 3))
        else:
            spread_mid, states = after(spread_mid, states, (1,))
            spread_mid, factors = after(spread_mid, factors, (4, 5, 2, 3, 6, 7, 1))
        normed_mid = exchange(spread_mid).reshape(tok_rows, width)
        if last:
            chosen = [
                choose(
                    n, sources, picks, init_state, own_part, in_order(states), in_order(parts),
                    pieces,
                )
                for n, (own_part, parts) in enumerate(((early_own, early), (own_factors, factors)))
            ]
            tied = lax.optimization_barrier((normed_mid, *chosen))
            normed_mid, chosen = tied[0], tied[1:]
        else:
            terms = feed(layer, pieces, normed_mid, w_up, w_down)
            terms, states = after(terms, states, (4,))
            terms, factors = after(terms, factors, (4, 5))
            stream, spread_rows = settle(exchange(terms), middle, norm_gain[layer + 1, 0])
            spread_rows, states = after(spread_rows, states, (5,))
            spread_rows, factors = after(spread_rows, factors, (2, 3, 6))
            normed = exchange(spread_rows).reshape(tok_rows, width)
            normed, states = after(normed, states, (6,))
            early, early_own = factors, own_factors
    piece = my_piece.astype(jnp.int32).reshape(1)
    landed = exchange(finish(LAYERS - 1, piece, normed_mid, middle, w_up, w_down, chosen))
    valid = valid_rows.astype(jnp.int32)[:, None]
    return deliver(landed, valid, home_shape)


def solution(mesh):
    in_specs = (
        P("req", "mlp"),
        P("req"),
        P("req"),
        P("req"),
        P(),
        P(None, "req", None, "mlp"),
        P(),
        P(None, None, "mlp"),
        P(None, None, "mlp"),
        P(None, None, "mlp"),
        P(None, None, "mlp"),
        P(None, "mlp", None),
        P(None, None, "mlp"),
        P(None, "mlp", None),
    )
    out_specs = (P("req", "mlp"), P(None, "req", "mlp", None))
    return jax.shard_map(shards, mesh=mesh, in_specs=in_specs, out_specs=out_specs, check_vma=False)
```
